32 devices in a mesh: dp: 2 (over y), hid: 4 (over x, core), wid: 4 (over z).
Axes of the slice: x: 2, y: 2, z: 4, core: 2. Of those that a mesh axis runs over, the one named last changes fastest.
Arguments:
- hidden_in: bfloat16 [6144, 1536], P('dp', 'wid'), may hold values from -6 to 6
- cotangent: bfloat16 [6144, 1536], P('dp', 'wid'), may hold values from -6 to 6
- segments: int32 [8, 768], P(('dp', 'wid')), may hold values from 0 to 2, never falling along the last dimension, each value on 1 to 512 neighbouring positions
- gain_attn: bfloat16 [1536], P(('dp', 'wid')), may hold values from 0.5 to 1.5
- gain_mlp: bfloat16 [1536], P(('dp', 'wid')), may hold values from 0.5 to 1.5
- in_weight: bfloat16 [1536, 4, 1536], P(('dp', 'wid'), None, 'hid'), may hold values from -0.15625 to 0.15625
- beta_weight: bfloat16 [1536, 12], P(('dp', 'wid'), 'hid'), may hold values from -0.15625 to 0.15625
- out_weight: bfloat16 [1536, 1536], P('hid', ('dp', 'wid')), may hold values from -2.5 to 2.5
- gate_weight: bfloat16 [1536, 4096], P(('dp', 'wid'), 'hid'), may hold values from -0.15625 to 0.15625
- up_weight: bfloat16 [1536, 4096], P(('dp', 'wid'), 'hid'), may hold values from -0.15625 to 0.15625
- down_weight: bfloat16 [4096, 1536], P('hid', ('dp', 'wid')), may hold values from -0.1875 to 0.1875
Outputs:
- output: bfloat16 [6144, 1536], P('dp', 'wid')
- grad_input: float32 [6144, 1536], P('dp', 'wid')
- grad_gain_attn: float32 [1536], P(('dp', 'wid'))
- grad_gain_mlp: float32 [1536], P(('dp', 'wid'))
- grad_in_weight: float32 [1536, 4, 1536], P(('dp', 'wid'), None, 'hid')
- grad_beta_weight: float32 [1536, 12], P(('dp', 'wid'), 'hid')
- grad_out_weight: float32 [1536, 1536], P('hid', ('dp', 'wid'))
- grad_gate_weight: float32 [1536, 4096], P(('dp', 'wid'), 'hid')
- grad_up_weight: float32 [1536, 4096], P(('dp', 'wid'), 'hid')
- grad_down_weight: float32 [4096, 1536], P('hid', ('dp', 'wid'))
The draws below stay inside these ranges and needn't reach their ends.
Inputs may be any that keep to these rules, and one draw needn't show every extreme that they name: `segments`: in each row (the 768 tokens of one block) ids never fall, each of the 3 ids occurs in one run of 1 to 512 tokens, and one run is exactly 512 long.
All inputs are finite; a program needn't handle non-finite values.
Results may differ from the reference program's by a relative error of at most 0.012.
The reference program's roundings to bfloat16 on the way count: a program that leaves them out, or rounds other values in their place, can miss the bound.
Values may be sent and summed in bfloat16 or wider, within the bound.
No kernel may reach another device: no remote copies, remote signals or barrier semaphores. Data moves between devices by JAX's collectives and lax.ppermute only.
A program may use at most 256 MiB of HBM per device.

```python
import math
import jax
import jax.numpy as jnp
import numpy as np
from jax import lax

D = 1536
H = 12
HD = 128
FF = 4096
TOK_DEV = 768
BLK = 64
SEQ_DEV = 3
MAX_LEN = 512
BLOCKS = 8
TOKENS = 6144


def block_levels(own_key, extent, cuts, least, largest):
    def one(axis_at, blocks):
        heights = jax.random.uniform(jax.random.fold_in(jax.random.fold_in(own_key, 6), axis_at), (blocks,), jnp.float32, least / len(cuts), largest / len(cuts))
        return jnp.repeat(jnp.exp(heights), extent[axis_at] // blocks).reshape((-1,) + (1,) * (len(extent) - axis_at - 1))

    loudness = one(*cuts[0])
    for cut in cuts[1:]:
        loudness = loudness * one(*cut)
    return loudness


def profile(count, total, limit, skew):
    loads = [(1 << 20) // math.isqrt(standing ** skew) + 1 for standing in range(2, count + 1)]
    spare, counts = total - limit - (count - 1), [1] * (count - 1)
    while spare > 0:
        free = [i for i in range(count - 1) if counts[i] < limit]
        mass, left = sum([loads[i] for i in free]), spare
        for i in free:
            extra = min(limit - counts[i], max(1, left * loads[i] // mass), spare)
            counts[i] = counts[i] + extra
            spare = spare - extra
    return np.array([limit] + counts)


def uneven_parts(rng, count, total, limit, lean):
    if count == 2:
        one = jax.random.randint(rng, (), max(1, total - limit), min(limit, total - 1) + 1)
        return jnp.stack([one, total - one])
    tallies = jnp.asarray(profile(count, total, limit, lean), jnp.int32)
    twos = (count - 1) // 2
    donor, sink = tallies[1:1 + 2 * twos:2], tallies[2:2 + 2 * twos:2]
    margin = jnp.minimum(donor - 1, limit - sink)
    moved = jax.random.randint(jax.random.fold_in(rng, 1), (twos,), 0, 1 << 20) % (margin + 1)
    tallies = tallies.at[1:1 + 2 * twos:2].set(donor - moved).at[2:2 + 2 * twos:2].set(sink + moved)
    return tallies[jax.random.permutation(jax.random.fold_in(rng, 2), count)]


def scatter_about(own_key, extent, width, bound, shards=(), kind=jnp.bfloat16):
    array = width * jax.random.normal(own_key, extent, jnp.float32)
    if shards:
        array = array * block_levels(own_key, extent, shards, -0.22, 0.18)
    return jnp.clip(array, -bound, bound).astype(kind)


def setup_inputs(seed: int = 0) -> dict:
    splits = jax.random.split(jax.random.key(seed), 12)
    hidden_in = scatter_about(splits[0], (TOKENS, D), 1.0, 6.0, ((0, 2), (1, 4)))
    cotangent = scatter_about(splits[1], (TOKENS, D), 1.0, 6.0, ((0, 2), (1, 4)))
    segments = jax.vmap(lambda own: jnp.searchsorted(jnp.cumsum(uneven_parts(own, SEQ_DEV, TOK_DEV, MAX_LEN, 0)), jnp.arange(TOK_DEV), side="right"))(jax.random.split(splits[2], BLOCKS)).reshape((BLOCKS, TOK_DEV)).astype(jnp.int32)
    gain_attn = jnp.clip(1.0 + 0.1 * jax.random.normal(splits[3], (D,), jnp.float32), 0.5, 1.5).astype(jnp.bfloat16)
    gain_mlp = jnp.clip(1.0 + 0.1 * jax.random.normal(splits[4], (D,), jnp.float32), 0.5, 1.5).astype(jnp.bfloat16)
    in_weight = scatter_about(splits[5], (D, 4, D), D ** -0.5, 0.15625, ((0, 8), (2, 4)))
    beta_weight = scatter_about(splits[6], (D, H), D ** -0.5, 0.15625, ((0, 8), (1, 4)))
    out_weight = scatter_about(splits[7], (D, D), (max(D // 256, 1)) ** -0.5, 2.5, ((0, 4), (1, 8)))
    gate_weight = scatter_about(splits[8], (D, FF), D ** -0.5, 0.15625, ((0, 8), (1, 4)))
    up_weight = scatter_about(splits[9], (D, FF), D ** -0.5, 0.15625, ((0, 8), (1, 4)))
    down_weight = scatter_about(splits[10], (FF, D), (FF // 4) ** -0.5, 0.1875, ((0, 4), (1, 8)))
    return {"hidden_in": hidden_in, "cotangent": cotangent, "segments": segments, "gain_attn": gain_attn, "gain_mlp": gain_mlp, "in_weight": in_weight, "beta_weight": beta_weight, "out_weight": out_weight, "gate_weight": gate_weight, "up_weight": up_weight, "down_weight": down_weight}


@jax.custom_vjp
def low(v):
    return lax.optimization_barrier(v.astype(jnp.bfloat16)).astype(jnp.float32)

@jax.custom_vjp
def low_back(v):
    return v

def low_keep(v):
    return (low(v), None)

def low_pass(kept, grad):
    return (grad,)

def back_keep(v):
    return (v, None)

def back_low(kept, grad):
    return (low(grad),)
low.defvjp(low_keep, low_pass)
low_back.defvjp(back_keep, back_low)

def householder_attention(queries, key_vecs, value_vecs, raw_dirs, beta_logit, segment_ids, block_size):
    highest = lax.Precision.HIGHEST
    length, head_count, head_width = queries.shape
    block_count = length // block_size
    directions = raw_dirs * lax.rsqrt(lax.optimization_barrier(jnp.sum(raw_dirs * raw_dirs, axis=-1, keepdims=True)) + 1e-06)
    strengths = 2.0 * jax.nn.sigmoid(beta_logit)
    query_blocks = queries.reshape(block_count, block_size, head_count, head_width)
    key_blocks = key_vecs.reshape(block_count, block_size, head_count, head_width)
    dir_blocks = directions.reshape(block_count, block_size, head_count, head_width)
    strength_blocks = strengths.reshape(block_count, block_size, head_count).transpose(0, 2, 1)
    offsets = jnp.arange(block_size)
    strict_lower = (offsets[:, None] > offsets[None, :]).astype(jnp.float32)
    lower_incl = (offsets[:, None] >= offsets[None, :]).astype(jnp.float32)
    identity = jnp.eye(block_size, dtype=jnp.float32)
    gram_matrix = jnp.einsum('nshd,nthd->nhst', dir_blocks, dir_blocks, precision=highest)
    system = identity + strength_blocks[..., :, None] * gram_matrix * strict_lower
    right_side = identity * strength_blocks[..., :, None]
    tri_factor = jax.scipy.linalg.solve_triangular(system, right_side, lower=True, unit_diagonal=True)
    query_dirs = jnp.einsum('nihd,nshd->nhis', query_blocks, dir_blocks, precision=highest) * lower_incl
    dir_keys = jnp.einsum('nthd,njhd->nhtj', dir_blocks, key_blocks, precision=highest) * strict_lower
    factor_keys = jnp.einsum('nhst,nhtj->nhsj', tri_factor, dir_keys, precision=highest)
    inner_scores = jnp.einsum('nihd,njhd->nhij', query_blocks, key_blocks, precision=highest)
    inner_scores = inner_scores - jnp.einsum('nhis,nhsj->nhij', query_dirs, factor_keys, precision=highest)
    keys_moved = key_blocks - jnp.einsum('nhsj,nshd->njhd', factor_keys, dir_blocks, precision=highest)
    query_factor = jnp.einsum('nhis,nhst->nhit', query_dirs, tri_factor, precision=highest)
    queries_moved = query_blocks - jnp.einsum('nhit,nthd->nihd', query_factor, dir_blocks, precision=highest)

    def sweep_step(moved_rows, item):
        block_index, keys_here, dirs_here, factor_here, inner_here, queries_here = item
        start = (block_index * block_size).astype(jnp.int32)
        zero_index = start * 0
        scores = jnp.einsum('ihd,jhd->hij', moved_rows, keys_here, precision=highest)
        scores = lax.dynamic_update_slice(scores, inner_here, (zero_index, start, zero_index))
        projected = jnp.einsum('ihd,shd->his', moved_rows, dirs_here, precision=highest)
        projected = jnp.einsum('his,hst->hit', projected, factor_here, precision=highest)
        moved_rows = moved_rows - jnp.einsum('hit,thd->ihd', projected, dirs_here, precision=highest)
        moved_rows = lax.dynamic_update_slice(moved_rows, queries_here, (start, zero_index, zero_index))
        return (moved_rows, scores)
    initial = jnp.zeros((length, head_count, head_width), jnp.float32)
    items = (jnp.arange(block_count, dtype=jnp.int32), keys_moved, dir_blocks, tri_factor, inner_scores, queries_moved)
    _, scores = lax.scan(jax.checkpoint(sweep_step), initial, items, reverse=True)
    scores = scores.transpose(1, 2, 0, 3).reshape(head_count, length, length)
    position = jnp.arange(length)
    allowed = (position[None, :] <= position[:, None]) & (segment_ids[:, None] == segment_ids[None, :])
    scores = jnp.where(allowed[None], scores * head_width ** (-0.5), -1e+30)
    row_top = lax.optimization_barrier(jnp.max(scores, axis=-1, keepdims=True))
    exponent = jnp.exp(scores - row_top)
    attn_probs = exponent / lax.optimization_barrier(jnp.sum(exponent, axis=-1, keepdims=True))
    return jnp.einsum('hij,jhd->ihd', attn_probs, value_vecs, precision=highest)

def rms_norm(values, gain):
    return values * lax.rsqrt(lax.optimization_barrier(jnp.mean(values * values, axis=-1, keepdims=True)) + 1e-06) * gain

def reference(hidden_in, cotangent, segments, gain_attn, gain_mlp, in_weight, beta_weight, out_weight, gate_weight, up_weight, down_weight):
    highest = lax.Precision.HIGHEST
    block_rows = segments.shape[1]

    def attend(items):
        pieces, logits, seg_row = items
        return householder_attention(pieces[:, 0], pieces[:, 1], pieces[:, 2], pieces[:, 3], logits, seg_row, BLK)
    attend_saved = jax.checkpoint(attend)

    def forward(inputs, gain_one, gain_two, weight_in, weight_beta, weight_out, weight_gate, weight_up, weight_down):
        normed = low(rms_norm(inputs, gain_one))
        projected = low_back(low(jnp.einsum('td,dkc->tkc', normed, weight_in, precision=highest)))
        logits = jnp.dot(normed, weight_beta, precision=highest)
        blocks = projected.reshape(-1, block_rows, 4, H, HD)
        block_logits = logits.reshape(-1, block_rows, H)
        attended = lax.map(attend_saved, (blocks, block_logits, segments))
        attended = low(attended.reshape(inputs.shape[0], H * HD))
        branch = low_back(jnp.dot(attended, weight_out, precision=highest))
        middle = inputs + branch
        mixed = low(rms_norm(middle, gain_two))
        gate = low_back(jnp.dot(mixed, weight_gate, precision=highest))
        upward = low_back(jnp.dot(mixed, weight_up, precision=highest))
        product = low(jax.nn.silu(gate) * upward)
        feed = low_back(jnp.dot(product, weight_down, precision=highest))
        return middle + feed
    primals = (hidden_in.astype(jnp.float32), gain_attn.astype(jnp.float32), gain_mlp.astype(jnp.float32), in_weight.astype(jnp.float32), beta_weight.astype(jnp.float32), out_weight.astype(jnp.float32), gate_weight.astype(jnp.float32), up_weight.astype(jnp.float32), down_weight.astype(jnp.float32))
    result, backward = jax.vjp(forward, primals[0], primals[1], primals[2], primals[3], primals[4], primals[5], primals[6], primals[7], primals[8])
    grads = backward(cotangent.astype(jnp.float32))
    return (result.astype(jnp.bfloat16), grads[0], grads[1], grads[2], grads[3], grads[4], grads[5], grads[6], grads[7], grads[8])
```

```python
import jax, jax.numpy as jnp
from jax import lax
from jax.experimental import pallas as pl
from jax.experimental.pallas import tpu as pltpu
from jax.sharding import PartitionSpec as P

HD = 128
F32 = jnp.float32
BF = jnp.bfloat16


def split(a):
    hi = a.astype(BF)
    return hi, (a - hi.astype(F32)).astype(BF)


def mm(a, b, ca, cb):
    dims = (((ca,), (cb,)), ((), ()))

    def one(x, y):
        return lax.dot_general(x, y, dims, preferred_element_type=F32)

    if isinstance(a, tuple) and isinstance(b, tuple):
        return one(a[0], b[0]) + (one(a[0], b[1]) + one(a[1], b[0]))
    if isinstance(a, tuple):
        return one(a[0], b) + one(a[1], b)
    if isinstance(b, tuple):
        return one(a, b[0]) + one(a, b[1])
    return one(a, b)


def beside(items):
    return tuple(jnp.concatenate([i[p] for i in items], axis=1) for p in range(2))


def cat(items):
    return tuple(jnp.concatenate([i[p] for i in items], axis=0) for p in range(2))


def grids(size):
    return (
        lax.broadcasted_iota(jnp.int32, (size, size), 0),
        lax.broadcasted_iota(jnp.int32, (size, size), 1),
    )


def to_col(row, eye):
    return jnp.sum(jnp.where(eye, row, 0.0), axis=1, keepdims=True)


def strengths(gram, logit_row, eye):
    square = jnp.where(eye, gram, 0.0)
    sig_row = 1.0 / (jnp.sum(square, axis=0, keepdims=True) + 1e-06)
    sig_col = 1.0 / (jnp.sum(square, axis=1, keepdims=True) + 1e-06)
    beta_row = 2.0 * jax.nn.sigmoid(logit_row)
    beta_col = to_col(beta_row, eye)
    return sig_row, sig_col, beta_row, beta_col


def inverses(lows, rows, cols, eye):
    invs = [jnp.where(eye, 1.0, jnp.where((rows ^ cols) == 1, -low, 0.0)) for low in lows]
    size = 2
    while size < rows.shape[0]:
        pair = (rows // size ^ cols // size) == 1
        parts = [split(inv) for inv in invs]
        offs = [split(jnp.where(pair, low, 0.0)) for low in lows]
        mids = [split(mm(off, part, 1, 0)) for off, part in zip(offs, parts)]
        invs = [inv - mm(part, mid, 1, 0) for inv, part, mid in zip(invs, parts, mids)]
        size *= 2
    return invs


def fwd_kernel(proj_ref, lg_ref, seg_ref, att_ref, pr_ref, qm_ref, x_ref, ft_ref, e_ref, kt_ref, p_ref, s_ref):
    length, width = att_ref.shape
    q_ref, k_ref, v_ref, r_ref = (proj_ref.at[:, n * width : (n + 1) * width] for n in range(4))
    blocks = length // width
    rows, cols = grids(width)
    eye = rows == cols
    lows, scales = [], []
    for c in range(blocks):
        r = r_ref[c * width : (c + 1) * width, :]
        gram = mm(r, r, 1, 1)
        sig_row, sig_col, beta_row, beta_col = strengths(gram, lg_ref[0, :, c * width : (c + 1) * width], eye)
        lows.append(jnp.where(rows > cols, gram * (beta_col * sig_col), 0.0))
        scales.append(beta_row * sig_row)
    invs = inverses(lows, rows, cols, eye)

    def chunk(c):
        at = pl.ds(pl.multiple_of(c * width, width), width)
        q, k, r = q_ref[at, :], k_ref[at, :], r_ref[at, :]
        prods = mm(jnp.concatenate([q, k], axis=0), r, 1, 1)
        qr, kr = prods[:width], prods[width : 2 * width]
        inv = invs[c]
        tri = split(inv * scales[c])
        qrl = split(jnp.where(rows >= cols, qr, 0.0))
        kru = split(jnp.where(rows < cols, kr, 0.0))
        ft = mm(kru, tri, 1, 1)
        e = mm(qrl, tri, 1, 0)
        fts, es = split(ft), split(e)
        moved = mm(cat([fts, es, tri]), r, 1, 0)
        s_ref[at, at] = mm(q, k, 1, 1) - mm(qrl, fts, 1, 1)
        kt_ref[0, at, :] = k.astype(F32) - moved[:width]
        qm_ref[0, c, at, :] = q.astype(F32) - moved[width : 2 * width]
        p_ref[0, at, :] = jnp.where(eye, 1.0, 0.0) - mm(r, split(moved[2 * width :]), 0, 0)
        x_ref[0, at, :] = inv
        ft_ref[0, at, :] = ft
        e_ref[0, at, :] = e

    for c in range(blocks):
        chunk(c)

    for j in range(blocks - 1, -1, -1):
        here = pl.ds(j * width, width)
        if j < blocks - 1:
            below = pl.ds((j + 1) * width, length - (j + 1) * width)
            moved = split(qm_ref[0, j, below, :])
            s_ref[below, here] = mm(moved, split(kt_ref[0, here, :]), 1, 1)
            if j:
                qm_ref[0, j - 1, below, :] = mm(moved, split(p_ref[0, here, :]), 1, 0)
        if j:
            qm_ref[0, j - 1, here, :] = qm_ref[0, j, here, :]

    seg_row = seg_ref[0:1, :].astype(F32)
    for i in range(blocks):
        here = pl.ds(i * width, width)
        upto = (i + 1) * width
        seg_col = to_col(seg_row[:, i * width : upto], eye)
        row = lax.broadcasted_iota(jnp.int32, (width, upto), 0) + i * width
        col = lax.broadcasted_iota(jnp.int32, (width, upto), 1)
        ok = (col <= row) & (seg_col == seg_row[:, :upto])
        score = jnp.where(ok, s_ref[here, :upto] * width ** (-0.5), -1e30)
        top = jnp.max(score, axis=1, keepdims=True)
        ex = jnp.exp(score - top)
        prob = ex / jnp.sum(ex, axis=1, keepdims=True)
        pr_ref[0, here, :upto] = prob
        att_ref[here, :] = mm(split(prob), v_ref[:upto, :], 1, 0).astype(att_ref.dtype)


def attend_fwd(proj, logits, seg):
    length, wide = proj.shape
    heads = wide // (4 * HD)
    blocks = length // HD
    part = pl.BlockSpec((length, 4 * HD), lambda h: (0, h))
    per = pl.BlockSpec((1, length, HD), lambda h: (h, 0, 0))
    st = jax.ShapeDtypeStruct
    return pl.pallas_call(
        fwd_kernel,
        grid=(heads,),
        in_specs=[part,
                  pl.BlockSpec((1, 1, length), lambda h: (h, 0, 0)),
                  pl.BlockSpec((1, length), lambda h: (0, 0))],
        out_specs=[pl.BlockSpec((length, HD), lambda h: (0, h)),
                   pl.BlockSpec((1, length, length), lambda h: (h, 0, 0)),
                   pl.BlockSpec((1, blocks, length, HD), lambda h: (h, 0, 0, 0)),
                   per, per, per, per, per],
        out_shape=[st((length, heads * HD), BF), st((heads, length, length), F32),
                   st((heads, blocks, length, HD), F32)] + [st((heads, length, HD), F32)] * 5,
        scratch_shapes=[pltpu.VMEM((length, length), F32)],
        compiler_params=pltpu.CompilerParams(vmem_limit_bytes=56 << 20, dimension_semantics=("arbitrary",)),
        name="attend_fwd",
    )(proj, logits.reshape(heads, 1, length), seg)


def bwd_kernel(proj_ref, lg_ref, do_ref, pr_ref, qm_ref, x_ref, ft_ref, e_ref, kt_ref, p_ref,
               dproj_ref, dl_ref, ds_ref, dkt_ref, dqt_ref, dp_ref):
    length, width = do_ref.shape
    q_ref, k_ref, v_ref, r_ref = (proj_ref.at[:, n * width : (n + 1) * width] for n in range(4))
    dq_ref, dk_ref, dv_ref, dr_ref = (dproj_ref.at[:, n * width : (n + 1) * width] for n in range(4))
    blocks = length // width
    rows, cols = grids(width)
    eye = rows == cols

    for i in range(blocks):
        here = pl.ds(i * width, width)
        upto = (i + 1) * width
        prob = pr_ref[0, here, :upto]
        dprob = mm(split(do_ref[here, :]), v_ref[:upto, :], 1, 1)
        delta = jnp.sum(prob * dprob, axis=1, keepdims=True)
        ds_ref[here, :upto] = prob * (dprob - delta) * width ** (-0.5)
    for j in range(blocks):
        here = pl.ds(j * width, width)
        below = pl.ds(j * width, length - j * width)
        dv_ref[here, :] = mm(split(pr_ref[0, below, here]), split(do_ref[below, :]), 0, 0).astype(dv_ref.dtype)

    zero = jnp.zeros((width, width), F32)
    dqt_ref[0:width, :] = zero
    dp_ref[0:width, :] = zero
    last = pl.ds((blocks - 1) * width, width)
    dkt_ref[last, :] = zero
    dp_ref[last, :] = zero
    grad = None
    for j in range(blocks - 1):
        here = pl.ds(j * width, width)
        below = pl.ds((j + 1) * width, length - (j + 1) * width)
        dsj = split(ds_ref[below, here])
        moved = split(qm_ref[0, j, below, :])
        dkt_ref[here, :] = mm(dsj, moved, 0, 0)
        fresh = mm(dsj, split(kt_ref[0, here, :]), 1, 0)
        if j:
            old = split(grad)
            dp_ref[here, :] = mm(moved, old, 0, 0)
            fresh = fresh + mm(old, split(p_ref[0, here, :]), 1, 1)
        dqt_ref[pl.ds((j + 1) * width, width), :] = fresh[:width]
        grad = fresh[width:]

    def chunk(c):
        at = pl.ds(pl.multiple_of(c * width, width), width)
        q, k, r = q_ref[at, :], k_ref[at, :], r_ref[at, :]
        prods = mm(jnp.concatenate([r, q, k], axis=0), r, 1, 1)
        gram, qr, kr = prods[:width], prods[width : 2 * width], prods[2 * width :]
        sig_row, sig_col, beta_row, beta_col = strengths(gram, lg_ref[0, :, at], eye)
        inv = x_ref[0, at, :]
        tri_full = inv * (beta_row * sig_row)
        tri = split(tri_full)
        qrl = split(jnp.where(rows >= cols, qr, 0.0))
        kru = split(jnp.where(rows < cols, kr, 0.0))
        ft, e = split(ft_ref[0, at, :]), split(e_ref[0, at, :])
        dsin = split(ds_ref[at, at])
        dkt_f, dqt_f = dkt_ref[at, :], dqt_ref[at, :]
        dkt, dqt = split(dkt_f), split(dqt_f)
        dp = split(dp_ref[at, :])
        y = split(mm(tri, r, 1, 0))
        dy = split(-mm(r, dp, 1, 0))
        both = mm(cat([dkt, dqt, dy]), r, 1, 1)
        dft = split(-both[:width] - mm(dsin, qrl, 0, 0))
        de = split(-both[width : 2 * width])
        dtri = both[2 * width :] + mm(cat([dft, qrl]), cat([kru, de]), 0, 0)
        dtris = split(dtri)
        dqr = split(jnp.where(rows >= cols, mm(de, tri, 1, 1) - mm(dsin, ft, 1, 0), 0.0))
        dkr = split(jnp.where(rows < cols, mm(dft, tri, 1, 0), 0.0))
        dlow = -mm(split(inv), split(mm(dtris, tri, 1, 1)), 0, 0)
        dlow = jnp.where(rows > cols, dlow, 0.0)
        b_col = beta_col * sig_col
        dgram = split(dlow * b_col)
        db = jnp.sum(dtri * inv, axis=0, keepdims=True)
        db_col = jnp.sum(dlow * gram, axis=1, keepdims=True)
        db = db + jnp.sum(jnp.where(eye, db_col, 0.0), axis=0, keepdims=True)
        dl_ref[0, :, at] = db * sig_row * beta_row * (1.0 - 0.5 * beta_row)
        dst = tuple(jnp.transpose(d) for d in dsin)
        dq = dqt_f + mm(beside([dsin, dqr]), jnp.concatenate([k, r], axis=0), 1, 0)
        dk = dkt_f + mm(beside([dst, dkr]), jnp.concatenate([q, r], axis=0), 1, 0)
        dr = mm(dgram, r, 1, 0) + mm(cat([dqr, dkr, dgram]), jnp.concatenate([q, k, r], axis=0), 0, 0)
        dr = dr - mm(cat([ft, e]), cat([dkt, dqt]), 0, 0) + mm(tri, dy, 0, 0) - mm(y, dp, 1, 1)
        dsig = to_col(db * beta_row, eye)
        dr = dr - (2.0 * dsig * sig_col * sig_col) * r.astype(F32)
        dq_ref[at, :] = dq.astype(dq_ref.dtype)
        dk_ref[at, :] = dk.astype(dk_ref.dtype)
        dr_ref[at, :] = dr.astype(dr_ref.dtype)

    for c in range(blocks):
        chunk(c)


def attend_bwd(proj, logits, saved, grad):
    length, wide = proj.shape
    heads = wide // (4 * HD)
    blocks = length // HD
    part = pl.BlockSpec((length, 4 * HD), lambda h: (0, h))
    per = pl.BlockSpec((1, length, HD), lambda h: (h, 0, 0))
    col = pl.BlockSpec((length, HD), lambda h: (0, h))
    lrow = pl.BlockSpec((1, 1, length), lambda h: (h, 0, 0))
    st = jax.ShapeDtypeStruct
    scr = pltpu.VMEM((length, HD), F32)
    return pl.pallas_call(
        bwd_kernel,
        grid=(heads,),
        in_specs=[part, lrow, col,
                  pl.BlockSpec((1, length, length), lambda h: (h, 0, 0)),
                  pl.BlockSpec((1, blocks, length, HD), lambda h: (h, 0, 0, 0)),
                  per, per, per, per, per],
        out_specs=[part, lrow],
        out_shape=[st((length, wide), BF), st((heads, 1, length), F32)],
        scratch_shapes=[pltpu.VMEM((length, length), F32), scr, scr, scr],
        compiler_params=pltpu.CompilerParams(vmem_limit_bytes=56 << 20, dimension_semantics=("arbitrary",)),
        name="attend_bwd",
    )(proj, logits.reshape(heads, 1, length), grad, *saved)


def after(value, *first):
    return lax.optimization_barrier((value,) + first)[0]


def shift(value, axis, size, by):
    return lax.ppermute(value, axis, [(i, (i + by) % size) for i in range(size)])


def swap(value, axis, size, bit):
    return lax.ppermute(value, axis, [(i, i ^ bit) for i in range(size)])


def norm_back(values, scale_row, gain, grad_out):
    weighted = grad_out * gain
    grad_gain = jnp.sum(grad_out * values * scale_row, axis=0)
    grad_values = scale_row * weighted - values * scale_row**3 * jnp.mean(
        weighted * values, axis=-1, keepdims=True
    )
    return (grad_gain, grad_values)


def make_body(sizes):
    dp, hid, wid = sizes["dp"], sizes["hid"], sizes["wid"]

    def body(
        hidden_in, cotangent, segments, gain_attn, gain_mlp,
        in_weight, beta_weight, out_weight, gate_weight, up_weight, down_weight,
    ):
        me_dp, me_hid, me_wid = (lax.axis_index(a) for a in ("dp", "hid", "wid"))
        tokens, slice_width = hidden_in.shape
        rows = tokens // wid
        quarter = rows // hid
        features = slice_width * wid
        heads = in_weight.shape[2] // HD
        shard = in_weight.shape[0]

        def dot(a, b, ca, cb, out=F32):
            return lax.dot_general(a, b, (((ca,), (cb,)), ((), ())), preferred_element_type=F32).astype(out)

        def to_tokens(array):
            mine = lax.dynamic_index_in_dim(array.reshape(wid, hid, quarter, slice_width), me_hid, 1, keepdims=False)
            return lax.all_to_all(mine.reshape(wid * quarter, slice_width), "wid", split_axis=0, concat_axis=1, tiled=True)

        def gather_hid(own):
            pieces = {0: own}
            bit = hid // 2
            while bit:
                for k in list(pieces):
                    pieces[k | bit] = swap(pieces[k], "hid", hid, bit)
                bit //= 2
            return [pieces[k] for k in range(hid)]

        def sum_hid(make):
            keep, bit = list(range(hid)), 1
            send = [k for k in keep if k & bit]
            keep = [k for k in keep if not k & bit]
            got = swap(make(send).astype(BF), "hid", hid, bit)
            total = make(keep) + got
            bit *= 2
            while bit < hid:
                half = total.shape[0] // 2
                low = [n for n, k in enumerate(keep) if not k & bit]
                high = [n for n, k in enumerate(keep) if k & bit]
                part = lambda ns: jnp.concatenate([total[n * quarter : (n + 1) * quarter] for n in ns], axis=0)
                got = swap(part(high).astype(BF), "hid", hid, bit)
                total = part(low) + got
                keep = [k for k in keep if not k & bit]
                bit *= 2
            return total

        def reorder(array, axis=0):
            size = array.shape[axis] // hid
            return jnp.concatenate(
                [lax.dynamic_slice_in_dim(array, (me_hid ^ j) * size, size, axis) for j in range(hid)], axis=axis
            )

        def gather_wid(own):
            return [own] + [shift(own, "wid", wid, k) for k in range(1, wid)]

        def gather_dp(pieces):
            got = [pieces] + [[shift(p, "dp", dp, k) for p in pieces] for k in range(1, dp)]
            cols = pieces[0].shape[1]
            whole = jnp.zeros((dp * wid, shard, cols), pieces[0].dtype)
            for i in range(dp):
                for k in range(wid):
                    place = ((me_dp + dp - i) % dp) * wid + (me_wid + wid - k) % wid
                    whole = lax.dynamic_update_slice(whole, got[i][k][None], (place, 0, 0))
            return whole.reshape(dp * wid * shard, cols)

        def scatter_grad(left, right):
            width = left.shape[1] // dp

            def part(k):
                cols = lax.dynamic_slice_in_dim(left, ((me_dp + k) % dp) * width, width, 1)
                return dot(cols, right, 0, 0)

            got = [shift(part(k).astype(BF), "dp", dp, k) for k in range(1, dp)]
            mine = part(0)
            for g in got:
                mine = mine + g
            parts = lax.all_to_all(mine.astype(BF), "wid", split_axis=0, concat_axis=0, tiled=True)
            return jnp.sum(parts.reshape(wid, shard, right.shape[1]).astype(F32), axis=0)

        def to_widths(own, dtype):
            mine = lax.all_to_all(own.astype(BF), "wid", split_axis=1, concat_axis=0, tiled=True)
            pieces = gather_hid(mine.reshape(wid, 1, quarter, slice_width))
            stacked = reorder(jnp.concatenate(pieces, axis=1), axis=1)
            return stacked.reshape(tokens, slice_width).astype(dtype)

        by_head = in_weight.reshape(shard, 4, heads, HD).transpose(0, 2, 1, 3).reshape(shard, 4 * heads * HD)
        small = jnp.concatenate([beta_weight, gain_attn[:, None], gain_mlp[:, None]], axis=1)
        small = jnp.pad(small, ((0, 0), (0, HD - small.shape[1])))
        own_in = jnp.concatenate([by_head, small], axis=1)
        own_mlp = jnp.concatenate([gate_weight, up_weight], axis=1)

        token_in = to_tokens(hidden_in)
        parts_in = gather_wid(own_in)
        inputs_all = jnp.concatenate(gather_hid(token_in), axis=0).astype(F32)
        parts_out = gather_wid(after(out_weight, *parts_in).T)
        weight_in = gather_dp(parts_in)
        parts_mlp = gather_wid(after(own_mlp, *parts_in))
        weight_out = gather_dp(parts_out)
        cotangent = after(cotangent, *parts_mlp)
        token_grad = to_tokens(cotangent)
        grad_all = jnp.concatenate(gather_hid(token_grad), axis=0)
        parts_down = gather_wid(after(down_weight, *parts_mlp).T)
        weight_mlp = gather_dp(parts_mlp)
        weight_down = gather_dp(parts_down)

        width_in = 4 * heads * HD
        weight_beta = weight_in[:, width_in : width_in + heads]
        gain_one = weight_in[:, width_in + heads].astype(F32)
        gain_two = weight_in[:, width_in + heads + 1].astype(F32)
        weight_in = weight_in[:, :width_in]

        scale_all = lax.rsqrt(jnp.mean(inputs_all * inputs_all, axis=-1, keepdims=True) + 1e-06)
        normed = (inputs_all * scale_all * gain_one).astype(BF)
        projected = reorder(dot(normed, weight_in, 1, 0, BF))
        logits = reorder(dot(normed, weight_beta, 1, 0)).T
        attended, *saved = attend_fwd(projected, logits, segments)
        attended = reorder(attended)

        def rows_of(array, ks):
            return jnp.concatenate([array[k * quarter : (k + 1) * quarter] for k in ks], axis=0)

        branch = sum_hid(lambda ks: dot(rows_of(attended, ks), weight_out, 1, 1))
        inputs = inputs_all[:quarter]
        scale_one = scale_all[:quarter]
        middle = inputs + branch
        scale_two = lax.rsqrt(jnp.mean(middle * middle, axis=-1, keepdims=True) + 1e-06)
        mixed = jnp.concatenate(gather_hid((middle * scale_two * gain_two).astype(BF)), axis=0)
        gate_up = dot(mixed, weight_mlp, 1, 0)
        hidden = gate_up.shape[1] // 2
        gate, upward = gate_up[:, :hidden], gate_up[:, hidden:]
        sigmoid_gate = jax.nn.sigmoid(gate)
        silu_gate = gate * sigmoid_gate
        product = (silu_gate * upward).astype(BF)

        grad_product = dot(grad_all, weight_down, 1, 0)
        grad_gate_pre = grad_product * upward * sigmoid_gate * (1.0 + gate * (1.0 - sigmoid_gate))
        grad_pre = jnp.concatenate([grad_gate_pre.astype(BF), (grad_product * silu_gate).astype(BF)], axis=1)
        grad_mixed = sum_hid(lambda ks: dot(rows_of(grad_pre, ks), weight_mlp, 1, 1))
        grad_down = scatter_grad(grad_all, product)
        grad_mlp = scatter_grad(mixed, grad_pre)

        grad_gain_two, grad_middle = norm_back(middle, scale_two, gain_two, grad_mixed)
        grad_middle = grad_middle + token_grad.astype(F32)
        grad_branch = jnp.concatenate(gather_hid(grad_middle.astype(BF)), axis=0)
        grad_attended = reorder(dot(grad_branch, weight_out, 1, 0))
        grad_proj, grad_logit = attend_bwd(projected, logits, saved, grad_attended)
        grad_out = scatter_grad(grad_branch, attended)

        feed = sum_hid(lambda ks: dot(rows_of(product, ks), weight_down, 1, 1))
        output = to_widths(middle + feed, BF)

        grad_proj = reorder(grad_proj)
        logit_parts = jnp.concatenate(split(reorder(grad_logit[:, 0, :].T)), axis=1)
        beta_twice = jnp.concatenate([weight_beta, weight_beta], axis=1)
        grad_normed = sum_hid(
            lambda ks: dot(rows_of(grad_proj, ks), weight_in, 1, 1) + dot(rows_of(logit_parts, ks), beta_twice, 1, 1)
        )
        grad_gain_one, grad_inputs = norm_back(inputs, scale_one, gain_one, grad_normed)
        grad_input = to_widths(grad_inputs + grad_middle, F32)
        grad_in = scatter_grad(normed, grad_proj)
        grad_beta = scatter_grad(normed, logit_parts)
        grad_beta = grad_beta[:, :heads] + grad_beta[:, heads:]
        grad_in = grad_in.reshape(shard, heads, 4, HD).transpose(0, 2, 1, 3).reshape(shard, 4, heads * HD)

        gains = lax.psum(jnp.stack([grad_gain_one, grad_gain_two]), ("dp", "hid", "wid"))
        gains = lax.dynamic_slice_in_dim(gains, (me_dp * wid + me_wid) * shard, shard, 1)
        return (
            output, grad_input, gains[0], gains[1], grad_in, grad_beta, grad_out.T,
            grad_mlp[:, :hidden], grad_mlp[:, hidden:], grad_down.T,
        )

    return body


def solution(mesh):
    by_rows, by_cols = P(("dp", "wid"), "hid"), P("hid", ("dp", "wid"))
    both = P(("dp", "wid"))
    deep = P(("dp", "wid"), None, "hid")
    wide = P("dp", "wid")
    return jax.shard_map(
        make_body(dict(mesh.shape)),
        mesh=mesh,
        in_specs=(wide, wide, P(("dp", "wid"), None), both, both, deep, by_rows, by_cols, by_rows, by_rows, by_cols),
        out_specs=(wide, wide, both, both, deep, by_rows, by_cols, by_rows, by_rows, by_cols),
        check_vma=False,
    )
```

```python
import functools
import jax, jax.numpy as jnp
from jax import lax
from jax.experimental import pallas as pl
from jax.experimental.pallas import tpu as pltpu
from jax.sharding import PartitionSpec as P

HD = 128
STEP = 64
F32 = jnp.float32
BF = jnp.bfloat16


def split(a):
    hi = a.astype(BF)
    return hi, (a - hi.astype(F32)).astype(BF)


def mm(a, b, ca, cb):
    dims = (((ca,), (cb,)), ((), ()))

    def one(x, y):
        return lax.dot_general(x, y, dims, preferred_element_type=F32)

    if isinstance(a, tuple) and isinstance(b, tuple):
        return one(a[0], b[0]) + (one(a[0], b[1]) + one(a[1], b[0]))
    if isinstance(a, tuple):
        return one(a[0], b) + one(a[1], b)
    if isinstance(b, tuple):
        return one(a, b[0]) + one(a, b[1])
    return one(a, b)


def beside(items):
    return tuple(jnp.concatenate([i[p] for i in items], axis=1) for p in range(2))


def cat(items):
    return tuple(jnp.concatenate([i[p] for i in items], axis=0) for p in range(2))


def grids(size):
    return (
        lax.broadcasted_iota(jnp.int32, (size, size), 0),
        lax.broadcasted_iota(jnp.int32, (size, size), 1),
    )


def to_col(row, eye):
    return jnp.sum(jnp.where(eye, row, 0.0), axis=1, keepdims=True)


def strengths(gram, logit_row, eye):
    square = jnp.where(eye, gram, 0.0)
    sig_row = 1.0 / (jnp.sum(square, axis=0, keepdims=True) + 1e-06)
    sig_col = 1.0 / (jnp.sum(square, axis=1, keepdims=True) + 1e-06)
    beta_row = 2.0 * jax.nn.sigmoid(logit_row)
    beta_col = to_col(beta_row, eye)
    return sig_row, sig_col, beta_row, beta_col


def inverses(lows, rows, cols, eye):
    invs = [jnp.where(eye, 1.0, jnp.where((rows ^ cols) == 1, -low, 0.0)) for low in lows]
    size = 2
    while size < rows.shape[0]:
        pair = (rows // size ^ cols // size) == 1
        parts = [split(inv) for inv in invs]
        offs = [split(jnp.where(pair, low, 0.0)) for low in lows]
        mids = [split(mm(off, part, 1, 0)) for off, part in zip(offs, parts)]
        invs = [inv - mm(part, mid, 1, 0) for inv, part, mid in zip(invs, parts, mids)]
        size *= 2
    return invs


def place_of(order_ref, block, per):
    return pl.ds(pl.multiple_of((((block // per) ^ order_ref[0]) * per + block % per) * STEP, STEP), STEP)


def fwd_kernel(per, order_ref, proj_ref, lg_ref, seg_ref, att_ref, pr_ref, qm_ref, x_ref, ft_ref, e_ref, kt_ref, p_ref, s_ref, own_ref):
    length, width = att_ref.shape
    for b in range(length // STEP):
        own_ref[b * STEP : (b + 1) * STEP, :] = proj_ref[place_of(order_ref, b, per), :]
    q_ref, k_ref, v_ref, r_ref = (own_ref.at[:, n * width : (n + 1) * width] for n in range(4))
    blocks = length // width
    rows, cols = grids(width)
    eye = rows == cols
    lows, scales = [], []
    for c in range(blocks):
        r = r_ref[c * width : (c + 1) * width, :]
        gram = mm(r, r, 1, 1)
        sig_row, sig_col, beta_row, beta_col = strengths(gram, lg_ref[0, :, c * width : (c + 1) * width], eye)
        lows.append(jnp.where(rows > cols, gram * (beta_col * sig_col), 0.0))
        scales.append(beta_row * sig_row)
    invs = inverses(lows, rows, cols, eye)

    def chunk(c):
        at = pl.ds(pl.multiple_of(c * width, width), width)
        q, k, r = q_ref[at, :], k_ref[at, :], r_ref[at, :]
        prods = mm(jnp.concatenate([q, k], axis=0), r, 1, 1)
        qr, kr = prods[:width], prods[width : 2 * width]
        inv = invs[c]
        tri = split(inv * scales[c])
        qrl = split(jnp.where(rows >= cols, qr, 0.0))
        kru = split(jnp.where(rows < cols, kr, 0.0))
        ft = mm(kru, tri, 1, 1)
        e = mm(qrl, tri, 1, 0)
        fts, es = split(ft), split(e)
        moved = mm(cat([fts, es, tri]), r, 1, 0)
        s_ref[at, at] = mm(q, k, 1, 1) - mm(qrl, fts, 1, 1)
        kt_ref[0, at, :] = k.astype(F32) - moved[:width]
        qm_ref[0, c, at, :] = q.astype(F32) - moved[width : 2 * width]
        p_ref[0, at, :] = jnp.where(eye, 1.0, 0.0) - mm(r, split(moved[2 * width :]), 0, 0)
        x_ref[0, at, :] = inv
        ft_ref[0, at, :] = ft
        e_ref[0, at, :] = e

    for c in range(blocks):
        chunk(c)

    for j in range(blocks - 1, -1, -1):
        here = pl.ds(j * width, width)
        if j < blocks - 1:
            below = pl.ds((j + 1) * width, length - (j + 1) * width)
            moved = split(qm_ref[0, j, below, :])
            s_ref[below, here] = mm(moved, split(kt_ref[0, here, :]), 1, 1)
            if j:
                qm_ref[0, j - 1, below, :] = mm(moved, split(p_ref[0, here, :]), 1, 0)
        if j:
            qm_ref[0, j - 1, here, :] = qm_ref[0, j, here, :]

    seg_row = seg_ref[0:1, :].astype(F32)
    for i in range(blocks):
        here = pl.ds(i * width, width)
        upto = (i + 1) * width
        seg_col = to_col(seg_row[:, i * width : upto], eye)
        row = lax.broadcasted_iota(jnp.int32, (width, upto), 0) + i * width
        col = lax.broadcasted_iota(jnp.int32, (width, upto), 1)
        ok = (col <= row) & (seg_col == seg_row[:, :upto])
        score = jnp.where(ok, s_ref[here, :upto] * width ** (-0.5), -1e30)
        top = jnp.max(score, axis=1, keepdims=True)
        ex = jnp.exp(score - top)
        prob = ex / jnp.sum(ex, axis=1, keepdims=True)
        pr_ref[0, here, :upto] = prob
        att = mm(split(prob), v_ref[:upto, :], 1, 0).astype(att_ref.dtype)
        for b in range(width // STEP):
            att_ref[place_of(order_ref, i * width // STEP + b, per), :] = att[b * STEP : (b + 1) * STEP]


def attend_fwd(order, proj, logits, seg, quarter):
    length, wide = proj.shape
    heads = wide // (4 * HD)
    blocks = length // HD
    part = pl.BlockSpec((length, 4 * HD), lambda h: (0, h))
    smem = pl.BlockSpec(memory_space=pltpu.SMEM)
    per = pl.BlockSpec((1, length, HD), lambda h: (h, 0, 0))
    st = jax.ShapeDtypeStruct
    return pl.pallas_call(
        functools.partial(fwd_kernel, quarter // STEP),
        grid=(heads,),
        in_specs=[smem, part,
                  pl.BlockSpec((1, 1, length), lambda h: (h, 0, 0)),
                  pl.BlockSpec((1, length), lambda h: (0, 0))],
        out_specs=[pl.BlockSpec((length, HD), lambda h: (0, h)),
                   pl.BlockSpec((1, length, length), lambda h: (h, 0, 0)),
                   pl.BlockSpec((1, blocks, length, HD), lambda h: (h, 0, 0, 0)),
                   per, per, per, per, per],
        out_shape=[st((length, heads * HD), BF), st((heads, length, length), F32),
                   st((heads, blocks, length, HD), F32)] + [st((heads, length, HD), F32)] * 5,
        scratch_shapes=[pltpu.VMEM((length, length), F32), pltpu.VMEM((length, 4 * HD), BF)],
        compiler_params=pltpu.CompilerParams(vmem_limit_bytes=56 << 20, dimension_semantics=("arbitrary",)),
        cost_estimate=pl.CostEstimate(flops=heads * 11 * 10**9, bytes_accessed=heads * 10**7, transcendentals=heads * length * length),
        name="attend_fwd",
    )(order, proj, logits.reshape(heads, 1, length), seg)


def bwd_kernel(per, order_ref, proj_ref, lg_ref, dog_ref, pr_ref, qm_ref, x_ref, ft_ref, e_ref, kt_ref, p_ref,
               dproj_ref, dl_ref, ds_ref, dkt_ref, dqt_ref, dp_ref, own_ref, do_ref, dv_ref):
    length, width = dog_ref.shape
    for b in range(length // STEP):
        rows = slice(b * STEP, (b + 1) * STEP)
        own_ref[rows, :] = proj_ref[place_of(order_ref, b, per), :]
        do_ref[rows, :] = dog_ref[place_of(order_ref, b, per), :]
    q_ref, k_ref, v_ref, r_ref = (own_ref.at[:, n * width : (n + 1) * width] for n in range(4))
    blocks = length // width
    rows, cols = grids(width)
    eye = rows == cols

    for i in range(blocks):
        here = pl.ds(i * width, width)
        upto = (i + 1) * width
        prob = pr_ref[0, here, :upto]
        dprob = mm(split(do_ref[here, :]), v_ref[:upto, :], 1, 1)
        delta = jnp.sum(prob * dprob, axis=1, keepdims=True)
        ds_ref[here, :upto] = prob * (dprob - delta) * width ** (-0.5)
    for j in range(blocks):
        here = pl.ds(j * width, width)
        below = pl.ds(j * width, length - j * width)
        dv_ref[here, :] = mm(split(pr_ref[0, below, here]), split(do_ref[below, :]), 0, 0)

    zero = jnp.zeros((width, width), F32)
    dqt_ref[0:width, :] = zero
    dp_ref[0:width, :] = zero
    last = pl.ds((blocks - 1) * width, width)
    dkt_ref[last, :] = zero
    dp_ref[last, :] = zero
    grad = None
    for j in range(blocks - 1):
        here = pl.ds(j * width, width)
        below = pl.ds((j + 1) * width, length - (j + 1) * width)
        dsj = split(ds_ref[below, here])
        moved = split(qm_ref[0, j, below, :])
        dkt_ref[here, :] = mm(dsj, moved, 0, 0)
        fresh = mm(dsj, split(kt_ref[0, here, :]), 1, 0)
        if j:
            old = split(grad)
            dp_ref[here, :] = mm(moved, old, 0, 0)
            fresh = fresh + mm(old, split(p_ref[0, here, :]), 1, 1)
        dqt_ref[pl.ds((j + 1) * width, width), :] = fresh[:width]
        grad = fresh[width:]

    def chunk(c):
        at = pl.ds(pl.multiple_of(c * width, width), width)
        q, k, r = q_ref[at, :], k_ref[at, :], r_ref[at, :]
        prods = mm(jnp.concatenate([r, q, k], axis=0), r, 1, 1)
        gram, qr, kr = prods[:width], prods[width : 2 * width], prods[2 * width :]
        sig_row, sig_col, beta_row, beta_col = strengths(gram, lg_ref[0, :, at], eye)
        inv = x_ref[0, at, :]
        tri_full = inv * (beta_row * sig_row)
        tri = split(tri_full)
        qrl = split(jnp.where(rows >= cols, qr, 0.0))
        kru = split(jnp.where(rows < cols, kr, 0.0))
        ft, e = split(ft_ref[0, at, :]), split(e_ref[0, at, :])
        dsin = split(ds_ref[at, at])
        dkt_f, dqt_f = dkt_ref[at, :], dqt_ref[at, :]
        dkt, dqt = split(dkt_f), split(dqt_f)
        dp = split(dp_ref[at, :])
        y = split(mm(tri, r, 1, 0))
        dy = split(-mm(r, dp, 1, 0))
        both = mm(cat([dkt, dqt, dy]), r, 1, 1)
        dft = split(-both[:width] - mm(dsin, qrl, 0, 0))
        de = split(-both[width : 2 * width])
        dtri = both[2 * width :] + mm(cat([dft, qrl]), cat([kru, de]), 0, 0)
        dtris = split(dtri)
        dqr = split(jnp.where(rows >= cols, mm(de, tri, 1, 1) - mm(dsin, ft, 1, 0), 0.0))
        dkr = split(jnp.where(rows < cols, mm(dft, tri, 1, 0), 0.0))
        dlow = -mm(split(inv), split(mm(dtris, tri, 1, 1)), 0, 0)
        dlow = jnp.where(rows > cols, dlow, 0.0)
        b_col = beta_col * sig_col
        dgram = split(dlow * b_col)
        db = jnp.sum(dtri * inv, axis=0, keepdims=True)
        db_col = jnp.sum(dlow * gram, axis=1, keepdims=True)
        db = db + jnp.sum(jnp.where(eye, db_col, 0.0), axis=0, keepdims=True)
        dl_ref[0, :, at] = db * sig_row * beta_row * (1.0 - 0.5 * beta_row)
        dst = tuple(jnp.transpose(d) for d in dsin)
        dq = dqt_f + mm(beside([dsin, dqr]), jnp.concatenate([k, r], axis=0), 1, 0)
        dk = dkt_f + mm(beside([dst, dkr]), jnp.concatenate([q, r], axis=0), 1, 0)
        dr = mm(dgram, r, 1, 0) + mm(cat([dqr, dkr, dgram]), jnp.concatenate([q, k, r], axis=0), 0, 0)
        dr = dr - mm(cat([ft, e]), cat([dkt, dqt]), 0, 0) + mm(tri, dy, 0, 0) - mm(y, dp, 1, 1)
        dsig = to_col(db * beta_row, eye)
        dr = dr - (2.0 * dsig * sig_col * sig_col) * r.astype(F32)
        whole = jnp.concatenate([dq, dk, dv_ref[at, :], dr], axis=1).astype(dproj_ref.dtype)
        for b in range(width // STEP):
            dproj_ref[place_of(order_ref, c * width // STEP + b, per), :] = whole[b * STEP : (b + 1) * STEP]

    for c in range(blocks):
        chunk(c)


def attend_bwd(order, proj, logits, saved, grad, quarter):
    length, wide = proj.shape
    heads = wide // (4 * HD)
    blocks = length // HD
    part = pl.BlockSpec((length, 4 * HD), lambda h: (0, h))
    smem = pl.BlockSpec(memory_space=pltpu.SMEM)
    per = pl.BlockSpec((1, length, HD), lambda h: (h, 0, 0))
    col = pl.BlockSpec((length, HD), lambda h: (0, h))
    lrow = pl.BlockSpec((1, 1, length), lambda h: (h, 0, 0))
    st = jax.ShapeDtypeStruct
    scr = pltpu.VMEM((length, HD), F32)
    return pl.pallas_call(
        functools.partial(bwd_kernel, quarter // STEP),
        grid=(heads,),
        in_specs=[smem, part, lrow, col,
                  pl.BlockSpec((1, length, length), lambda h: (h, 0, 0)),
                  pl.BlockSpec((1, blocks, length, HD), lambda h: (h, 0, 0, 0)),
                  per, per, per, per, per],
        out_specs=[part, lrow],
        out_shape=[st((length, wide), BF), st((heads, 1, length), F32)],
        scratch_shapes=[pltpu.VMEM((length, length), F32), scr, scr, scr, pltpu.VMEM((length, 4 * HD), BF), scr, scr],
        compiler_params=pltpu.CompilerParams(vmem_limit_bytes=56 << 20, dimension_semantics=("arbitrary",)),
        cost_estimate=pl.CostEstimate(flops=15 * 10**9, bytes_accessed=10**7, transcendentals=length),
        name="attend_bwd",
    )(order, proj, logits.reshape(heads, 1, length), grad, *saved)


def assemble(pieces, places, widths):
    size, count = pieces[0].shape[0], len(pieces)

    def kernel(place_ref, *refs):
        for n in range(count):
            rows = pl.ds(pl.multiple_of(place_ref[n] * size, size), size)
            start = 0
            for out, width in zip(refs[count:], widths):
                out[rows, :] = refs[n][:, start : start + width]
                start += width

    vmem = pl.BlockSpec(memory_space=pltpu.VMEM)
    return pl.pallas_call(
        kernel,
        in_specs=[pl.BlockSpec(memory_space=pltpu.SMEM)] + [vmem] * count,
        out_specs=[vmem] * len(widths),
        out_shape=[jax.ShapeDtypeStruct((count * size, w), BF) for w in widths],
        compiler_params=pltpu.CompilerParams(vmem_limit_bytes=56 << 20),
        cost_estimate=pl.CostEstimate(flops=0, bytes_accessed=4 * count * size * sum(widths), transcendentals=0),
        name="assemble",
    )(jnp.stack(places), *pieces)


def after(value, *first):
    return lax.optimization_barrier((value,) + first)[0]


class Lane:
    def __init__(self, depth):
        self.depth, self.done = depth, []

    def send(self, value, axis, pairs, *first):
        if len(self.done) >= self.depth:
            first = first + (self.done[-self.depth],)
        if first:
            value = after(value, *first)
        self.done.append(lax.ppermute(value, axis, pairs))
        return self.done[-1]


class Flow:
    def __init__(self, make):
        self.make, self.got, self.sent, self.out = make, None, None, None

    def step(self, *first):
        try:
            self.sent, self.got = self.make.send(first) if self.got is not None else next(self.make)
        except StopIteration as end:
            self.out = end.value
        return self.got

    def finish(self, *first):
        while self.out is None:
            self.step(*first)
        return self.out


def norm_back(values, scale_row, gain, grad_out):
    weighted = grad_out * gain
    grad_gain = jnp.sum(grad_out * values * scale_row, axis=0)
    grad_values = scale_row * weighted - values * scale_row**3 * jnp.mean(
        weighted * values, axis=-1, keepdims=True
    )
    return (grad_gain, grad_values)


def make_body(sizes):
    dp, hid, wid = sizes["dp"], sizes["hid"], sizes["wid"]

    def body(
        hidden_in, cotangent, segments, gain_attn, gain_mlp,
        in_weight, beta_weight, out_weight, gate_weight, up_weight, down_weight,
    ):
        me_dp, me_hid, me_wid = (lax.axis_index(a) for a in ("dp", "hid", "wid"))
        tokens, slice_width = hidden_in.shape
        rows = tokens // wid
        quarter = rows // hid
        heads = in_weight.shape[2] // HD
        shard = in_weight.shape[0]
        lane_x, lane_y, lane_z = Lane(4), Lane(6), Lane(4)

        def dot(a, b, ca, cb, out=F32):
            return lax.dot_general(a, b, (((ca,), (cb,)), ((), ())), preferred_element_type=F32).astype(out)

        def swap(value, bit, *first):
            return lane_x.send(value, "hid", [(i, i ^ bit) for i in range(hid)], *first)

        def to_tokens(array):
            mine = lax.dynamic_index_in_dim(array.reshape(wid, hid, quarter, slice_width), me_hid, 1, keepdims=False)
            return lax.all_to_all(mine.reshape(wid * quarter, slice_width), "wid", split_axis=0, concat_axis=1, tiled=True)

        def gather_hid(own):
            pieces = {0: own}
            bit = hid // 2
            while bit:
                for k in list(pieces):
                    pieces[k | bit] = swap(pieces[k], bit)
                bit //= 2
            return [pieces[k] for k in range(hid)]

        def summing_hid(make, first=()):
            keep, bit = list(range(hid)), 1
            send = [k for k in keep if k & bit]
            keep = [k for k in keep if not k & bit]
            sent = make(send).astype(BF)
            got = swap(sent, bit, *first)
            wait = yield sent, got
            total = make(keep) + (after(got, *wait) if wait else got)
            bit *= 2
            while bit < hid:
                low = [n for n, k in enumerate(keep) if not k & bit]
                high = [n for n, k in enumerate(keep) if k & bit]
                part = lambda ns: jnp.concatenate([total[n * quarter : (n + 1) * quarter] for n in ns], axis=0)
                sent = part(high).astype(BF)
                got = swap(sent, bit)
                wait = yield sent, got
                total = part(low) + (after(got, *wait) if wait else got)
                keep = [k for k in keep if not k & bit]
                bit *= 2
            return total

        def sum_hid(make):
            return Flow(summing_hid(make)).finish()

        def reorder(array, axis=0):
            size = array.shape[axis] // hid
            return jnp.concatenate(
                [lax.dynamic_slice_in_dim(array, (me_hid ^ j) * size, size, axis) for j in range(hid)], axis=axis
            )

        def rows_of(array, ks):
            return jnp.concatenate([array[k * quarter : (k + 1) * quarter] for k in ks], axis=0)

        def scattering(make, kept, wid_first=False, first=()):
            def bits(size):
                return [1 << n for n in range(size.bit_length() - 1)]

            def over(axis, lane, parts, bit, first):
                high = [j for j in parts if j & bit]
                sent = jnp.concatenate([parts[j].astype(BF) for j in high], axis=0)
                got = lane.send(sent, axis, [(i, i ^ bit) for i in range(sizes[axis])], *first)
                wait = yield sent, got
                got = after(got, *wait) if wait else got
                low = [j for j in parts if not j & bit]
                size = sent.shape[0] // len(high)
                return {j: parts[j] + got[n * size : (n + 1) * size] for n, j in enumerate(low)}, ()

            parts = {j: make(j) for j in range(dp)}
            kept.append(parts[0])
            if not wid_first:
                for bit in reversed(bits(dp)):
                    parts, first = yield from over("dp", lane_y, parts, bit, first)
            width = parts[0].shape[-1]
            blocks = {j: part.reshape(wid, shard, width) for j, part in parts.items()}
            parts = {
                n: jnp.concatenate([lax.dynamic_index_in_dim(b, me_wid ^ n, 0, keepdims=False) for b in blocks.values()], axis=0)
                for n in range(wid)
            }
            for bit in bits(wid):
                parts, first = yield from over("wid", lane_z, parts, bit, first)
            if wid_first:
                parts = dict(enumerate(jnp.split(parts[0], dp, axis=0)))
                for bit in reversed(bits(dp)):
                    parts, first = yield from over("dp", lane_y, parts, bit, first)
            return parts[0]

        def scatter_grad(left, right, first=(), kept=None):
            kept = [] if kept is None else kept
            return Flow(scattering(lambda by: dot(half(left, by), right, 0, 0), kept, False, first))

        def half(left, by):
            width = left.shape[1] // dp
            return lax.dynamic_slice_in_dim(left, (me_dp ^ by) * width, width, 1)

        def to_widths(own, *first):
            mine = lax.all_to_all(after(own.astype(BF), *first), "wid", split_axis=1, concat_axis=0, tiled=True)
            return mine.reshape(wid, 1, own.shape[0], slice_width)

        def placed(pieces, dtype):
            stacked = reorder(jnp.concatenate([p[:, :, :quarter] for p in pieces], axis=1), axis=1)
            return stacked.reshape(tokens, slice_width).astype(dtype)

        inner, hidden = out_weight.shape[0], gate_weight.shape[1]

        def gather_rows(own):
            return lax.all_gather(own, ("dp", "wid"), axis=0, tiled=True)

        weight_out = gather_rows(out_weight.T)

        hops = list(range(wid))
        hops = [0, 1] + hops[:1:-1] if wid > 2 else hops

        def along_wid(own, *first):
            if first:
                own = after(own, *first)
            made = [own]
            for k in hops[1:]:
                sent = own if k in (1, wid - 1) else after(own, *made[1:])
                made.append(lax.ppermute(sent, "wid", [(i, (i + k) % wid) for i in range(wid)]))
            return made

        def over_dp(piece, *first):
            return [piece] + [lane_y.send(piece, "dp", [(i, (i + by) % dp) for i in range(dp)], *first) for by in range(1, dp)]

        def whole(pieces, widths):
            places = [
                (me_dp + dp - by) % dp * wid + (me_wid + wid - k) % wid for k in hops for by in range(dp)
            ]
            return assemble([p for ps in pieces for p in ps], places, widths)

        token_in = to_tokens(hidden_in)
        width_in = 4 * heads * HD
        columns = [in_weight[:, c, h * HD : (h + 1) * HD] for h in range(heads) for c in range(4)]
        small = [beta_weight, gain_attn[:, None], gain_mlp[:, None], jnp.zeros((shard, HD - heads - 2), BF)]
        along = along_wid(jnp.concatenate(columns + small, axis=1))
        own_late = jnp.concatenate([gate_weight, up_weight, down_weight.T], axis=1)
        inputs_all = jnp.concatenate(gather_hid(token_in), axis=0).astype(F32)
        pieces = [over_dp(a) for a in along]
        late_along = along_wid(own_late, along[-1])
        late = [over_dp(own_late)]
        weight_in, small = whole(pieces, (width_in, HD))
        weight_beta = small[:, :heads]
        gain_one = small[:, heads].astype(F32)
        gain_two = small[:, heads + 1].astype(F32)

        scale_all = lax.rsqrt(jnp.mean(inputs_all * inputs_all, axis=-1, keepdims=True) + 1e-06)
        normed = (inputs_all * scale_all * gain_one).astype(BF)
        projected = dot(normed, weight_in, 1, 0, BF)
        order = me_hid.reshape(1)
        logits = reorder(dot(normed, weight_beta, 1, 0)).T
        late += [over_dp(a) for a in late_along[1:]]
        attended, *saved = attend_fwd(order, after(projected, *late_along[1:3]), logits, segments, quarter)
        attended = after(attended, late[1][-1])
        token_grad = to_tokens(after(cotangent, attended))

        branch_flow = Flow(summing_hid(lambda ks: dot(rows_of(attended, ks), weight_out, 1, 1)))
        branch_flow.step()
        branch_flow.step(late_along[-1])
        branch = branch_flow.finish(late[2][-1])
        inputs = inputs_all[:quarter]
        scale_one = scale_all[:quarter]
        middle = inputs + branch
        scale_two = lax.rsqrt(jnp.mean(middle * middle, axis=-1, keepdims=True) + 1e-06)
        mixed = jnp.concatenate(gather_hid((middle * scale_two * gain_two).astype(BF)), axis=0)
        grad_all = jnp.concatenate(gather_hid(after(token_grad, mixed)), axis=0)
        weight_mlp, weight_down = whole(late, (2 * hidden, hidden))
        gate_up = dot(mixed, weight_mlp, 1, 0)
        gate, upward = gate_up[:, :hidden], gate_up[:, hidden:]
        sigmoid_gate = jax.nn.sigmoid(gate)
        silu_gate = gate * sigmoid_gate
        product = (silu_gate * upward).astype(BF)
        def scatter_plain(full):
            return lax.psum_scatter(full, ("dp", "wid"), scatter_dimension=0, tiled=True).astype(F32)

        down_full = dot(grad_all, product, 0, 0, BF)
        grad_down = scatter_plain(down_full)
        grad_product = dot(grad_all, weight_down, 1, 0)
        grad_gate_pre = grad_product * upward * sigmoid_gate * (1.0 + gate * (1.0 - sigmoid_gate))
        grad_gate_pre, grad_up_pre = grad_gate_pre.astype(BF), (grad_product * silu_gate).astype(BF)
        kept = [down_full]
        gate_flow, up_flow = (scatter_grad(mixed, g, kept=kept) for g in (grad_gate_pre, grad_up_pre))
        grad_pre = jnp.concatenate([grad_gate_pre, grad_up_pre], axis=1)
        mixed_flow = Flow(summing_hid(lambda ks: dot(rows_of(grad_pre, ks), weight_mlp, 1, 1)))
        mixed_flow.step()
        gate_flow.step()
        mixed_flow.step()
        feed_flow = Flow(summing_hid(lambda ks: dot(rows_of(product, ks), weight_down, 1, 1)))
        feed_flow.step()
        grad_mixed = mixed_flow.finish()
        up_flow.step()
        grad_gain_two, grad_middle = norm_back(middle, scale_two, gain_two, grad_mixed)
        grad_middle = grad_middle + token_grad.astype(F32)
        quarters = gather_hid(grad_middle.astype(BF))
        grad_branch = after(jnp.concatenate(quarters, axis=0), gate_flow.got, *kept)
        grad_attended = dot(grad_branch, weight_out, 1, 0)
        gate_flow.step(grad_branch)
        feed_flow.step(grad_branch)

        grad_proj, grad_logit = attend_bwd(order, projected, logits, saved, grad_attended, quarter)
        grad_proj = after(grad_proj, up_flow.got, feed_flow.got)
        grad_logit = grad_logit[:, 0, :]
        logit_parts = jnp.concatenate(split(reorder(grad_logit, axis=1)), axis=0)
        beta_twice = jnp.concatenate([weight_beta, weight_beta], axis=1)

        def back(ks):
            lower = jnp.concatenate([logit_parts[:, k * quarter : (k + 1) * quarter] for k in ks], axis=1)
            return dot(rows_of(grad_proj, ks), weight_in, 1, 1) + dot(lower, beta_twice, 0, 1)

        back_flow = Flow(summing_hid(back))
        back_flow.step()
        begun = back_flow.sent
        in_flow = scatter_grad(normed, after(grad_proj, begun))
        in_flow.step()
        up_flow.step(begun)
        feed_widths = to_widths(middle + feed_flow.finish(begun))
        back_flow.step()
        handed = back_flow.sent
        grad_normed = back_flow.finish()
        gate_flow.step(handed)
        grad_gain_one, grad_inputs = norm_back(inputs, scale_one, gain_one, grad_normed)
        grad_beta = dot(after(logit_parts, handed), normed, 1, 0)
        grad_beta = grad_beta[:heads] + grad_beta[heads:]
        vectors = jnp.concatenate([grad_gain_one[None], grad_gain_two[None], grad_beta], axis=0)
        count = vectors.shape[0]
        vectors = vectors.reshape(count, dp, wid, shard).transpose(0, 2, 1, 3).reshape(count, wid * dp * shard)
        extra = jnp.concatenate(split(vectors), axis=0)
        extra = jnp.pad(extra, ((0, -(2 * count) % 16), (0, 0)))
        ended = jnp.concatenate([(grad_inputs + grad_middle).astype(BF), extra], axis=0)
        grad_widths = to_widths(ended)
        in_flow.step(ended)
        up_flow.step(grad_widths)
        grad_out = scatter_plain(dot(grad_branch, after(attended, handed), 0, 0, BF))
        out_pieces = gather_hid(after(feed_widths, ended))
        in_pieces = gather_hid(grad_widths)
        arrived = in_pieces[hid // 2]
        in_flow.step(grad_widths)
        passed = in_flow.sent
        grad_gate, grad_up = gate_flow.finish(arrived), up_flow.finish(passed)

        def row_sums(piece):
            both = jnp.sum(piece[:, 0, quarter : quarter + 2 * count].astype(F32), axis=0)
            return (both[:count] + both[count:]).reshape(count, dp, shard)

        sums = [row_sums(p) for p in in_pieces]
        gains = functools.reduce(jnp.add, [one[:2] for one in sums])
        sums = jnp.concatenate([gains, sums[0][2:]], axis=0)
        vectors = lax.dynamic_index_in_dim(sums, me_dp, 1, keepdims=False)
        for by in range(1, dp):
            theirs = lax.dynamic_index_in_dim(sums, (me_dp + by) % dp, 1, keepdims=False)
            vectors = vectors + lax.ppermute(theirs, "dp", [(i, (i + by) % dp) for i in range(dp)])
        in_pieces = [after(p, passed) for p in in_pieces]
        output, grad_input = placed(out_pieces, BF), placed(in_pieces, F32)
        grad_in = in_flow.finish().reshape(shard, heads, 4, HD).transpose(0, 2, 1, 3).reshape(shard, 4, heads * HD)

        return (
            output, grad_input, vectors[0], vectors[1], grad_in, vectors[2:].T, grad_out.T,
            grad_gate, grad_up, grad_down.T,
        )

    return body


def solution(mesh):
    by_rows, by_cols = P(("dp", "wid"), "hid"), P("hid", ("dp", "wid"))
    both = P(("dp", "wid"))
    deep = P(("dp", "wid"), None, "hid")
    wide = P("dp", "wid")
    return jax.shard_map(
        make_body(dict(mesh.shape)),
        mesh=mesh,
        in_specs=(wide, wide, P(("dp", "wid"), None), both, both, deep, by_rows, by_cols, by_rows, by_rows, by_cols),
        out_specs=(wide, wide, both, both, deep, by_rows, by_cols, by_rows, by_rows, by_cols),
        check_vma=False,
    )
```

```python
import functools
import jax, jax.numpy as jnp
from jax import lax
from jax.experimental import pallas as pl
from jax.experimental.pallas import tpu as pltpu
from jax.sharding import PartitionSpec as P

HD = 128
STEP = 64
F32 = jnp.float32
BF = jnp.bfloat16


def split(a):
    hi = a.astype(BF)
    return hi, (a - hi.astype(F32)).astype(BF)


def mm(a, b, ca, cb):
    dims = (((ca,), (cb,)), ((), ()))

    def one(x, y):
        return lax.dot_general(x, y, dims, preferred_element_type=F32)

    if isinstance(a, tuple) and isinstance(b, tuple):
        return one(a[0], b[0]) + (one(a[0], b[1]) + one(a[1], b[0]))
    if isinstance(a, tuple):
        return one(a[0], b) + one(a[1], b)
    if isinstance(b, tuple):
        return one(a, b[0]) + one(a, b[1])
    return one(a, b)


def beside(items):
    return tuple(jnp.concatenate([i[p] for i in items], axis=1) for p in range(2))


def cat(items):
    return tuple(jnp.concatenate([i[p] for i in items], axis=0) for p in range(2))


def grids(size):
    return (
        lax.broadcasted_iota(jnp.int32, (size, size), 0),
        lax.broadcasted_iota(jnp.int32, (size, size), 1),
    )


def to_col(row, eye):
    return jnp.sum(jnp.where(eye, row, 0.0), axis=1, keepdims=True)


def strengths(gram, logit_row, eye):
    square = jnp.where(eye, gram, 0.0)
    sig_row = 1.0 / (jnp.sum(square, axis=0, keepdims=True) + 1e-06)
    sig_col = 1.0 / (jnp.sum(square, axis=1, keepdims=True) + 1e-06)
    beta_row = 2.0 * jax.nn.sigmoid(logit_row)
    beta_col = to_col(beta_row, eye)
    return sig_row, sig_col, beta_row, beta_col


def inverses(lows, rows, cols, eye):
    invs = [jnp.where(eye, 1.0, jnp.where((rows ^ cols) == 1, -low, 0.0)) for low in lows]
    size = 2
    while size < rows.shape[0]:
        pair = (rows // size ^ cols // size) == 1
        parts = [split(inv) for inv in invs]
        offs = [split(jnp.where(pair, low, 0.0)) for low in lows]
        mids = [split(mm(off, part, 1, 0)) for off, part in zip(offs, parts)]
        invs = [inv - mm(part, mid, 1, 0) for inv, part, mid in zip(invs, parts, mids)]
        size *= 2
    return invs


def place_of(order_ref, block, per):
    return pl.ds(pl.multiple_of((((block // per) ^ order_ref[0]) * per + block % per) * STEP, STEP), STEP)


def fwd_kernel(per, order_ref, proj_ref, lg_ref, seg_ref, att_ref, pr_ref, qm_ref, x_ref, ft_ref, e_ref, kt_ref, p_ref, s_ref, own_ref):
    length, width = att_ref.shape
    for b in range(length // STEP):
        own_ref[b * STEP : (b + 1) * STEP, :] = proj_ref[place_of(order_ref, b, per), :]
    q_ref, k_ref, v_ref, r_ref = (own_ref.at[:, n * width : (n + 1) * width] for n in range(4))
    blocks = length // width
    rows, cols = grids(width)
    eye = rows == cols
    lows, scales = [], []
    for c in range(blocks):
        r = r_ref[c * width : (c + 1) * width, :]
        gram = mm(r, r, 1, 1)
        sig_row, sig_col, beta_row, beta_col = strengths(gram, lg_ref[0, :, c * width : (c + 1) * width], eye)
        lows.append(jnp.where(rows > cols, gram * (beta_col * sig_col), 0.0))
        scales.append(beta_row * sig_row)
    invs = inverses(lows, rows, cols, eye)

    def chunk(c):
        at = pl.ds(pl.multiple_of(c * width, width), width)
        q, k, r = q_ref[at, :], k_ref[at, :], r_ref[at, :]
        prods = mm(jnp.concatenate([q, k], axis=0), r, 1, 1)
        qr, kr = prods[:width], prods[width : 2 * width]
        inv = invs[c]
        tri = split(inv * scales[c])
        qrl = split(jnp.where(rows >= cols, qr, 0.0))
        kru = split(jnp.where(rows < cols, kr, 0.0))
        ft = mm(kru, tri, 1, 1)
        e = mm(qrl, tri, 1, 0)
        fts, es = split(ft), split(e)
        moved = mm(cat([fts, es, tri]), r, 1, 0)
        s_ref[at, at] = mm(q, k, 1, 1) - mm(qrl, fts, 1, 1)
        kt_ref[0, at, :] = k.astype(F32) - moved[:width]
        qm_ref[0, c, at, :] = q.astype(F32) - moved[width : 2 * width]
        p_ref[0, at, :] = jnp.where(eye, 1.0, 0.0) - mm(r, split(moved[2 * width :]), 0, 0)
        x_ref[0, at, :] = inv
        ft_ref[0, at, :] = ft
        e_ref[0, at, :] = e

    for c in range(blocks):
        chunk(c)

    for j in range(blocks - 1, -1, -1):
        here = pl.ds(j * width, width)
        if j < blocks - 1:
            below = pl.ds((j + 1) * width, length - (j + 1) * width)
            moved = split(qm_ref[0, j, below, :])
            s_ref[below, here] = mm(moved, split(kt_ref[0, here, :]), 1, 1)
            if j:
                qm_ref[0, j - 1, below, :] = mm(moved, split(p_ref[0, here, :]), 1, 0)
        if j:
            qm_ref[0, j - 1, here, :] = qm_ref[0, j, here, :]

    seg_row = seg_ref[0:1, :].astype(F32)
    for i in range(blocks):
        here = pl.ds(i * width, width)
        upto = (i + 1) * width
        seg_col = to_col(seg_row[:, i * width : upto], eye)
        row = lax.broadcasted_iota(jnp.int32, (width, upto), 0) + i * width
        col = lax.broadcasted_iota(jnp.int32, (width, upto), 1)
        ok = (col <= row) & (seg_col == seg_row[:, :upto])
        score = jnp.where(ok, s_ref[here, :upto] * width ** (-0.5), -1e30)
        top = jnp.max(score, axis=1, keepdims=True)
        ex = jnp.exp(score - top)
        prob = ex / jnp.sum(ex, axis=1, keepdims=True)
        pr_ref[0, here, :upto] = prob
        att = mm(split(prob), v_ref[:upto, :], 1, 0).astype(att_ref.dtype)
        for b in range(width // STEP):
            att_ref[place_of(order_ref, i * width // STEP + b, per), :] = att[b * STEP : (b + 1) * STEP]


def attend_fwd(order, proj, logits, seg, quarter):
    length, wide = proj.shape
    heads = wide // (4 * HD)
    blocks = length // HD
    part = pl.BlockSpec((length, 4 * HD), lambda h: (0, h))
    smem = pl.BlockSpec(memory_space=pltpu.SMEM)
    per = pl.BlockSpec((1, length, HD), lambda h: (h, 0, 0))
    st = jax.ShapeDtypeStruct
    return pl.pallas_call(
        functools.partial(fwd_kernel, quarter // STEP),
        grid=(heads,),
        in_specs=[smem, part,
                  pl.BlockSpec((1, 1, length), lambda h: (h, 0, 0)),
                  pl.BlockSpec((1, length), lambda h: (0, 0))],
        out_specs=[pl.BlockSpec((length, HD), lambda h: (0, h)),
                   pl.BlockSpec((1, length, length), lambda h: (h, 0, 0)),
                   pl.BlockSpec((1, blocks, length, HD), lambda h: (h, 0, 0, 0)),
                   per, per, per, per, per],
        out_shape=[st((length, heads * HD), BF), st((heads, length, length), F32),
                   st((heads, blocks, length, HD), F32)] + [st((heads, length, HD), F32)] * 5,
        scratch_shapes=[pltpu.VMEM((length, length), F32), pltpu.VMEM((length, 4 * HD), BF)],
        compiler_params=pltpu.CompilerParams(vmem_limit_bytes=56 << 20, dimension_semantics=("arbitrary",)),
        cost_estimate=pl.CostEstimate(flops=heads * 11 * 10**9, bytes_accessed=heads * 10**7, transcendentals=heads * length * length),
        name="attend_fwd",
    )(order, proj, logits.reshape(heads, 1, length), seg)


def bwd_kernel(per, order_ref, proj_ref, lg_ref, dog_ref, pr_ref, qm_ref, x_ref, ft_ref, e_ref, kt_ref, p_ref,
               dproj_ref, dl_ref, ds_ref, dkt_ref, dqt_ref, dp_ref, own_ref, do_ref, dv_ref):
    length, width = dog_ref.shape
    for b in range(length // STEP):
        rows = slice(b * STEP, (b + 1) * STEP)
        own_ref[rows, :] = proj_ref[place_of(order_ref, b, per), :]
        do_ref[rows, :] = dog_ref[place_of(order_ref, b, per), :]
    q_ref, k_ref, v_ref, r_ref = (own_ref.at[:, n * width : (n + 1) * width] for n in range(4))
    blocks = length // width
    rows, cols = grids(width)
    eye = rows == cols

    for i in range(blocks):
        here = pl.ds(i * width, width)
        upto = (i + 1) * width
        prob = pr_ref[0, here, :upto]
        dprob = mm(split(do_ref[here, :]), v_ref[:upto, :], 1, 1)
        delta = jnp.sum(prob * dprob, axis=1, keepdims=True)
        ds_ref[here, :upto] = prob * (dprob - delta) * width ** (-0.5)
    for j in range(blocks):
        here = pl.ds(j * width, width)
        below = pl.ds(j * width, length - j * width)
        dv_ref[here, :] = mm(split(pr_ref[0, below, here]), split(do_ref[below, :]), 0, 0)

    zero = jnp.zeros((width, width), F32)
    dqt_ref[0:width, :] = zero
    dp_ref[0:width, :] = zero
    last = pl.ds((blocks - 1) * width, width)
    dkt_ref[last, :] = zero
    dp_ref[last, :] = zero
    grad = None
    for j in range(blocks - 1):
        here = pl.ds(j * width, width)
        below = pl.ds((j + 1) * width, length - (j + 1) * width)
        dsj = split(ds_ref[below, here])
        moved = split(qm_ref[0, j, below, :])
        dkt_ref[here, :] = mm(dsj, moved, 0, 0)
        fresh = mm(dsj, split(kt_ref[0, here, :]), 1, 0)
        if j:
            old = split(grad)
            dp_ref[here, :] = mm(moved, old, 0, 0)
            fresh = fresh + mm(old, split(p_ref[0, here, :]), 1, 1)
        dqt_ref[pl.ds((j + 1) * width, width), :] = fresh[:width]
        grad = fresh[width:]

    def chunk(c):
        at = pl.ds(pl.multiple_of(c * width, width), width)
        q, k, r = q_ref[at, :], k_ref[at, :], r_ref[at, :]
        prods = mm(jnp.concatenate([r, q, k], axis=0), r, 1, 1)
        gram, qr, kr = prods[:width], prods[width : 2 * width], prods[2 * width :]
        sig_row, sig_col, beta_row, beta_col = strengths(gram, lg_ref[0, :, at], eye)
        inv = x_ref[0, at, :]
        tri_full = inv * (beta_row * sig_row)
        tri = split(tri_full)
        qrl = split(jnp.where(rows >= cols, qr, 0.0))
        kru = split(jnp.where(rows < cols, kr, 0.0))
        ft, e = split(ft_ref[0, at, :]), split(e_ref[0, at, :])
        dsin = split(ds_ref[at, at])
        dkt_f, dqt_f = dkt_ref[at, :], dqt_ref[at, :]
        dkt, dqt = split(dkt_f), split(dqt_f)
        dp = split(dp_ref[at, :])
        y = split(mm(tri, r, 1, 0))
        dy = split(-mm(r, dp, 1, 0))
        both = mm(cat([dkt, dqt, dy]), r, 1, 1)
        dft = split(-both[:width] - mm(dsin, qrl, 0, 0))
        de = split(-both[width : 2 * width])
        dtri = both[2 * width :] + mm(cat([dft, qrl]), cat([kru, de]), 0, 0)
        dtris = split(dtri)
        dqr = split(jnp.where(rows >= cols, mm(de, tri, 1, 1) - mm(dsin, ft, 1, 0), 0.0))
        dkr = split(jnp.where(rows < cols, mm(dft, tri, 1, 0), 0.0))
        dlow = -mm(split(inv), split(mm(dtris, tri, 1, 1)), 0, 0)
        dlow = jnp.where(rows > cols, dlow, 0.0)
        b_col = beta_col * sig_col
        dgram = split(dlow * b_col)
        db = jnp.sum(dtri * inv, axis=0, keepdims=True)
        db_col = jnp.sum(dlow * gram, axis=1, keepdims=True)
        db = db + jnp.sum(jnp.where(eye, db_col, 0.0), axis=0, keepdims=True)
        dl_ref[0, :, at] = db * sig_row * beta_row * (1.0 - 0.5 * beta_row)
        dst = tuple(jnp.transpose(d) for d in dsin)
        dq = dqt_f + mm(beside([dsin, dqr]), jnp.concatenate([k, r], axis=0), 1, 0)
        dk = dkt_f + mm(beside([dst, dkr]), jnp.concatenate([q, r], axis=0), 1, 0)
        dr = mm(dgram, r, 1, 0) + mm(cat([dqr, dkr, dgram]), jnp.concatenate([q, k, r], axis=0), 0, 0)
        dr = dr - mm(cat([ft, e]), cat([dkt, dqt]), 0, 0) + mm(tri, dy, 0, 0) - mm(y, dp, 1, 1)
        dsig = to_col(db * beta_row, eye)
        dr = dr - (2.0 * dsig * sig_col * sig_col) * r.astype(F32)
        whole = jnp.concatenate([dq, dk, dv_ref[at, :], dr], axis=1).astype(dproj_ref.dtype)
        for b in range(width // STEP):
            dproj_ref[place_of(order_ref, c * width // STEP + b, per), :] = whole[b * STEP : (b + 1) * STEP]

    for c in range(blocks):
        chunk(c)


def attend_bwd(order, proj, logits, saved, grad, quarter):
    length, wide = proj.shape
    heads = wide // (4 * HD)
    blocks = length // HD
    part = pl.BlockSpec((length, 4 * HD), lambda h: (0, h))
    smem = pl.BlockSpec(memory_space=pltpu.SMEM)
    per = pl.BlockSpec((1, length, HD), lambda h: (h, 0, 0))
    col = pl.BlockSpec((length, HD), lambda h: (0, h))
    lrow = pl.BlockSpec((1, 1, length), lambda h: (h, 0, 0))
    st = jax.ShapeDtypeStruct
    scr = pltpu.VMEM((length, HD), F32)
    return pl.pallas_call(
        functools.partial(bwd_kernel, quarter // STEP),
        grid=(heads,),
        in_specs=[smem, part, lrow, col,
                  pl.BlockSpec((1, length, length), lambda h: (h, 0, 0)),
                  pl.BlockSpec((1, blocks, length, HD), lambda h: (h, 0, 0, 0)),
                  per, per, per, per, per],
        out_specs=[part, lrow],
        out_shape=[st((length, wide), BF), st((heads, 1, length), F32)],
        scratch_shapes=[pltpu.VMEM((length, length), F32), scr, scr, scr, pltpu.VMEM((length, 4 * HD), BF), scr, scr],
        compiler_params=pltpu.CompilerParams(vmem_limit_bytes=56 << 20, dimension_semantics=("arbitrary",)),
        cost_estimate=pl.CostEstimate(flops=15 * 10**9, bytes_accessed=10**7, transcendentals=length),
        name="attend_bwd",
    )(order, proj, logits.reshape(heads, 1, length), grad, *saved)


def assemble(pieces, places, widths):
    size, count = pieces[0].shape[0], len(pieces)

    def kernel(place_ref, *refs):
        for n in range(count):
            rows = pl.ds(pl.multiple_of(place_ref[n] * size, size), size)
            start = 0
            for out, width in zip(refs[count:], widths):
                out[rows, :] = refs[n][:, start : start + width]
                start += width

    vmem = pl.BlockSpec(memory_space=pltpu.VMEM)
    return pl.pallas_call(
        kernel,
        in_specs=[pl.BlockSpec(memory_space=pltpu.SMEM)] + [vmem] * count,
        out_specs=[vmem] * len(widths),
        out_shape=[jax.ShapeDtypeStruct((count * size, w), BF) for w in widths],
        compiler_params=pltpu.CompilerParams(vmem_limit_bytes=56 << 20),
        cost_estimate=pl.CostEstimate(flops=0, bytes_accessed=4 * count * size * sum(widths), transcendentals=0),
        name="assemble",
    )(jnp.stack(places), *pieces)


def after(value, *first):
    return lax.optimization_barrier((value,) + first)[0]


class Lane:
    def __init__(self, depth):
        self.depth, self.done = depth, []

    def send(self, value, axis, pairs, *first):
        if len(self.done) >= self.depth:
            first = first + (self.done[-self.depth],)
        if first:
            value = after(value, *first)
        self.done.append(lax.ppermute(value, axis, pairs))
        return self.done[-1]


class Flow:
    def __init__(self, make):
        self.make, self.got, self.sent, self.out = make, None, None, None

    def step(self, *first):
        try:
            self.sent, self.got = self.make.send(first) if self.got is not None else next(self.make)
        except StopIteration as end:
            self.out = end.value
        return self.got

    def finish(self, *first):
        while self.out is None:
            self.step(*first)
        return self.out


def norm_back(values, scale_row, gain, grad_out):
    weighted = grad_out * gain
    grad_gain = jnp.sum(grad_out * values * scale_row, axis=0)
    grad_values = scale_row * weighted - values * scale_row**3 * jnp.mean(
        weighted * values, axis=-1, keepdims=True
    )
    return (grad_gain, grad_values)


def make_body(sizes):
    dp, hid, wid = sizes["dp"], sizes["hid"], sizes["wid"]

    def body(
        hidden_in, cotangent, segments, gain_attn, gain_mlp,
        in_weight, beta_weight, out_weight, gate_weight, up_weight, down_weight,
    ):
        me_dp, me_hid, me_wid = (lax.axis_index(a) for a in ("dp", "hid", "wid"))
        tokens, slice_width = hidden_in.shape
        rows = tokens // wid
        quarter = rows // hid
        heads = in_weight.shape[2] // HD
        shard = in_weight.shape[0]
        lane_x, lane_y, lane_z = Lane(4), Lane(6), Lane(4)

        def dot(a, b, ca, cb, out=F32):
            return lax.dot_general(a, b, (((ca,), (cb,)), ((), ())), preferred_element_type=F32).astype(out)

        def swap(value, bit, *first):
            return lane_x.send(value, "hid", [(i, i ^ bit) for i in range(hid)], *first)

        def to_tokens(array):
            mine = lax.dynamic_index_in_dim(array.reshape(wid, hid, quarter, slice_width), me_hid, 1, keepdims=False)
            return lax.all_to_all(mine.reshape(wid * quarter, slice_width), "wid", split_axis=0, concat_axis=1, tiled=True)

        def gather_hid(own):
            pieces = {0: own}
            bit = hid // 2
            while bit:
                for k in list(pieces):
                    pieces[k | bit] = swap(pieces[k], bit)
                bit //= 2
            return [pieces[k] for k in range(hid)]

        def summing_hid(make, first=()):
            keep, bit = list(range(hid)), 1
            send = [k for k in keep if k & bit]
            keep = [k for k in keep if not k & bit]
            sent = make(send).astype(BF)
            got = swap(sent, bit, *first)
            wait = yield sent, got
            total = make(keep) + (after(got, *wait) if wait else got)
            bit *= 2
            while bit < hid:
                low = [n for n, k in enumerate(keep) if not k & bit]
                high = [n for n, k in enumerate(keep) if k & bit]
                part = lambda ns: jnp.concatenate([total[n * quarter : (n + 1) * quarter] for n in ns], axis=0)
                sent = part(high).astype(BF)
                got = swap(sent, bit)
                wait = yield sent, got
                total = part(low) + (after(got, *wait) if wait else got)
                keep = [k for k in keep if not k & bit]
                bit *= 2
            return total

        def sum_hid(make):
            return Flow(summing_hid(make)).finish()

        def reorder(array, axis=0):
            size = array.shape[axis] // hid
            return jnp.concatenate(
                [lax.dynamic_slice_in_dim(array, (me_hid ^ j) * size, size, axis) for j in range(hid)], axis=axis
            )

        def rows_of(array, ks):
            return jnp.concatenate([array[k * quarter : (k + 1) * quarter] for k in ks], axis=0)

        def scattering(make, kept, wid_first=False, first=()):
            def bits(size):
                return [1 << n for n in range(size.bit_length() - 1)]

            def over(axis, lane, parts, bit, first):
                high = [j for j in parts if j & bit]
                sent = jnp.concatenate([parts[j].astype(BF) for j in high], axis=0)
                got = lane.send(sent, axis, [(i, i ^ bit) for i in range(sizes[axis])], *first)
                wait = yield sent, got
                got = after(got, *wait) if wait else got
                low = [j for j in parts if not j & bit]
                size = sent.shape[0] // len(high)
                return {j: parts[j] + got[n * size : (n + 1) * size] for n, j in enumerate(low)}, ()

            parts = {j: make(j) for j in range(dp)}
            kept.append(parts[0])
            if not wid_first:
                for bit in reversed(bits(dp)):
                    parts, first = yield from over("dp", lane_y, parts, bit, first)
            width = parts[0].shape[-1]
            blocks = {j: part.reshape(wid, shard, width) for j, part in parts.items()}
            parts = {
                n: jnp.concatenate([lax.dynamic_index_in_dim(b, me_wid ^ n, 0, keepdims=False) for b in blocks.values()], axis=0)
                for n in range(wid)
            }
            for bit in bits(wid):
                parts, first = yield from over("wid", lane_z, parts, bit, first)
            if wid_first:
                parts = dict(enumerate(jnp.split(parts[0], dp, axis=0)))
                for bit in reversed(bits(dp)):
                    parts, first = yield from over("dp", lane_y, parts, bit, first)
            return parts[0]

        def scatter_grad(left, right, first=(), kept=None):
            kept = [] if kept is None else kept
            return Flow(scattering(lambda by: dot(half(left, by), right, 0, 0), kept, False, first))

        def half(left, by):
            width = left.shape[1] // dp
            return lax.dynamic_slice_in_dim(left, (me_dp ^ by) * width, width, 1)

        def to_widths(own, *first):
            mine = lax.all_to_all(after(own.astype(BF), *first), "wid", split_axis=1, concat_axis=0, tiled=True)
            return mine.reshape(wid, 1, own.shape[0], slice_width)

        def placed(pieces, dtype):
            stacked = reorder(jnp.concatenate([p[:, :, :quarter] for p in pieces], axis=1), axis=1)
            return stacked.reshape(tokens, slice_width).astype(dtype)

        inner, hidden = out_weight.shape[0], gate_weight.shape[1]

        def gather_rows(own):
            return lax.all_gather(own, ("dp", "wid"), axis=0, tiled=True)

        weight_out = gather_rows(out_weight.T)

        hops = list(range(wid))
        hops = [0, 1] + hops[:1:-1] if wid > 2 else hops

        def hop(own, k, *first):
            return lax.ppermute(after(own, *first) if first else own, "wid", [(i, (i + k) % wid) for i in range(wid)])

        def over_dp(piece, *first):
            return [piece] + [lane_y.send(piece, "dp", [(i, (i + by) % dp) for i in range(dp)], *first) for by in range(1, dp)]

        def whole(pieces, widths):
            places = [
                (me_dp + dp - by) % dp * wid + (me_wid + wid - k) % wid for k in hops for by in range(dp)
            ]
            return assemble([p for ps in pieces for p in ps], places, widths)

        token_in = to_tokens(hidden_in)
        width_in = 4 * heads * HD
        columns = [in_weight[:, c, h * HD : (h + 1) * HD] for h in range(heads) for c in range(4)]
        small = [beta_weight, gain_attn[:, None], gain_mlp[:, None], jnp.zeros((shard, HD - heads - 2), BF)]
        own_in = jnp.concatenate(columns + small, axis=1)
        own_late = jnp.concatenate([gate_weight, up_weight, down_weight.T], axis=1)
        along = [own_in] + [hop(own_in, k) for k in hops[1:3]]
        pieces = [over_dp(own_in)]
        tokens_hid = gather_hid(token_in)
        along = along[:1] + [after(a, token_in) for a in along[1:]]
        for k in hops[3:]:
            along.append(hop(own_in, k, *along[1:], pieces[0][-1], tokens_hid[hid // 2]))
        inputs_all = jnp.concatenate(tokens_hid, axis=0).astype(F32)
        pieces += [over_dp(a) for a in along[1:]]
        late_along = [own_late] + [hop(own_late, k, along[-1]) for k in hops[1:3]]
        late = [over_dp(own_late)]
        weight_in, small = whole(pieces, (width_in, HD))
        weight_beta = small[:, :heads]
        gain_one = small[:, heads].astype(F32)
        gain_two = small[:, heads + 1].astype(F32)

        scale_all = lax.rsqrt(jnp.mean(inputs_all * inputs_all, axis=-1, keepdims=True) + 1e-06)
        normed = (inputs_all * scale_all * gain_one).astype(BF)
        projected = dot(after(normed, late[0][-1]), weight_in, 1, 0, BF)
        order = me_hid.reshape(1)
        logits = reorder(dot(normed, weight_beta, 1, 0)).T
        for k in hops[3:]:
            late_along.append(hop(own_late, k, *late_along[1:]))
        late += [over_dp(a) for a in late_along[1:3]]
        token_grad = to_tokens(after(cotangent, projected))
        attended, *saved = attend_fwd(order, after(projected, *late_along[1:3]), logits, segments, quarter)
        attended = after(attended, late[1][-1], token_grad)

        branch_flow = Flow(summing_hid(lambda ks: dot(rows_of(attended, ks), weight_out, 1, 1)))
        branch_flow.step()
        branch_flow.step(*late_along[3:])
        branch = branch_flow.finish(late[2][-1])
        late += [over_dp(a) for a in late_along[3:]]
        inputs = inputs_all[:quarter]
        scale_one = scale_all[:quarter]
        middle = inputs + branch
        scale_two = lax.rsqrt(jnp.mean(middle * middle, axis=-1, keepdims=True) + 1e-06)
        mixed_own = (middle * scale_two * gain_two).astype(BF)
        mixed = gather_hid(mixed_own)
        mixed = jnp.concatenate(mixed[:-1] + [after(mixed[-1], late[-1][-1])], axis=0)
        grad_all = jnp.concatenate(gather_hid(after(token_grad, mixed_own)), axis=0)
        weight_mlp, weight_down = whole(late, (2 * hidden, hidden))
        gate_up = dot(mixed, weight_mlp, 1, 0)
        gate, upward = gate_up[:, :hidden], gate_up[:, hidden:]
        sigmoid_gate = jax.nn.sigmoid(gate)
        silu_gate = gate * sigmoid_gate
        product = (silu_gate * upward).astype(BF)
        def scatter_plain(full):
            return lax.psum_scatter(full, ("dp", "wid"), scatter_dimension=0, tiled=True).astype(F32)

        down_full = dot(grad_all, product, 0, 0, BF)
        grad_down = scatter_plain(down_full)
        grad_product = dot(grad_all, weight_down, 1, 0)
        grad_gate_pre = grad_product * upward * sigmoid_gate * (1.0 + gate * (1.0 - sigmoid_gate))
        grad_gate_pre, grad_up_pre = grad_gate_pre.astype(BF), (grad_product * silu_gate).astype(BF)
        kept = [down_full]
        gate_flow, up_flow = (scatter_grad(mixed, g, kept=kept) for g in (grad_gate_pre, grad_up_pre))
        grad_pre = jnp.concatenate([grad_gate_pre, grad_up_pre], axis=1)
        mixed_flow = Flow(summing_hid(lambda ks: dot(rows_of(grad_pre, ks), weight_mlp, 1, 1)))
        mixed_flow.step()
        gate_flow.step()
        mixed_flow.step()
        feed_flow = Flow(summing_hid(lambda ks: dot(rows_of(product, ks), weight_down, 1, 1)))
        feed_flow.step()
        grad_mixed = mixed_flow.finish()
        up_flow.step()
        grad_gain_two, grad_middle = norm_back(middle, scale_two, gain_two, grad_mixed)
        grad_middle = grad_middle + token_grad.astype(F32)
        quarters = gather_hid(grad_middle.astype(BF))
        grad_branch = after(jnp.concatenate(quarters, axis=0), gate_flow.got, *kept)
        grad_attended = dot(grad_branch, weight_out, 1, 0)
        gate_flow.step(grad_branch)
        feed_flow.step(grad_branch)

        grad_proj, grad_logit = attend_bwd(order, projected, logits, saved, grad_attended, quarter)
        grad_proj = after(grad_proj, up_flow.got, feed_flow.got)
        grad_logit = grad_logit[:, 0, :]
        logit_parts = jnp.concatenate(split(reorder(grad_logit, axis=1)), axis=0)
        beta_twice = jnp.concatenate([weight_beta, weight_beta], axis=1)

        def back(ks):
            lower = jnp.concatenate([logit_parts[:, k * quarter : (k + 1) * quarter] for k in ks], axis=1)
            return dot(rows_of(grad_proj, ks), weight_in, 1, 1) + dot(lower, beta_twice, 0, 1)

        back_flow = Flow(summing_hid(back))
        back_flow.step()
        begun = back_flow.sent
        in_flow = scatter_grad(normed, after(grad_proj, begun))
        in_flow.step()
        up_flow.step(begun)
        feed_widths = to_widths(middle + feed_flow.finish(begun))
        back_flow.step()
        handed = back_flow.sent
        grad_normed = back_flow.finish()
        gate_flow.step(handed)
        grad_gain_one, grad_inputs = norm_back(inputs, scale_one, gain_one, grad_normed)
        grad_beta = dot(after(logit_parts, handed), normed, 1, 0)
        grad_beta = grad_beta[:heads] + grad_beta[heads:]
        vectors = jnp.concatenate([grad_gain_one[None], grad_gain_two[None], grad_beta], axis=0)
        count = vectors.shape[0]
        vectors = vectors.reshape(count, dp, wid, shard).transpose(0, 2, 1, 3).reshape(count, wid * dp * shard)
        extra = jnp.concatenate(split(vectors), axis=0)
        extra = jnp.pad(extra, ((0, -(2 * count) % 16), (0, 0)))
        ended = jnp.concatenate([(grad_inputs + grad_middle).astype(BF), extra], axis=0)
        grad_widths = to_widths(ended)
        in_flow.step(ended)
        up_flow.step(grad_widths)
        grad_out = scatter_plain(dot(grad_branch, after(attended, handed), 0, 0, BF))
        out_pieces = gather_hid(after(feed_widths, ended))
        in_pieces = gather_hid(grad_widths)
        arrived = in_pieces[hid // 2]
        in_flow.step(grad_widths)
        passed = in_flow.sent
        grad_gate, grad_up = gate_flow.finish(arrived), up_flow.finish(passed)

        def row_sums(piece):
            both = jnp.sum(piece[:, 0, quarter : quarter + 2 * count].astype(F32), axis=0)
            return (both[:count] + both[count:]).reshape(count, dp, shard)

        sums = [row_sums(p) for p in in_pieces]
        gains = functools.reduce(jnp.add, [one[:2] for one in sums])
        sums = jnp.concatenate([gains, sums[0][2:]], axis=0)
        vectors = lax.dynamic_index_in_dim(sums, me_dp, 1, keepdims=False)
        for by in range(1, dp):
            theirs = lax.dynamic_index_in_dim(sums, (me_dp + by) % dp, 1, keepdims=False)
            vectors = vectors + lax.ppermute(theirs, "dp", [(i, (i + by) % dp) for i in range(dp)])
        in_pieces = [after(p, passed) for p in in_pieces]
        output, grad_input = placed(out_pieces, BF), placed(in_pieces, F32)
        grad_in = in_flow.finish().reshape(shard, heads, 4, HD).transpose(0, 2, 1, 3).reshape(shard, 4, heads * HD)

        return (
            output, grad_input, vectors[0], vectors[1], grad_in, vectors[2:].T, grad_out.T,
            grad_gate, grad_up, grad_down.T,
        )

    return body


def solution(mesh):
    by_rows, by_cols = P(("dp", "wid"), "hid"), P("hid", ("dp", "wid"))
    both = P(("dp", "wid"))
    deep = P(("dp", "wid"), None, "hid")
    wide = P("dp", "wid")
    return jax.shard_map(
        make_body(dict(mesh.shape)),
        mesh=mesh,
        in_specs=(wide, wide, P(("dp", "wid"), None), both, both, deep, by_rows, by_cols, by_rows, by_rows, by_cols),
        out_specs=(wide, wide, both, both, deep, by_rows, by_cols, by_rows, by_rows, by_cols),
        check_vma=False,
    )
```

```python
import functools
import jax, jax.numpy as jnp
from jax import lax
from jax.experimental import pallas as pl
from jax.experimental.pallas import tpu as pltpu
from jax.sharding import PartitionSpec as P

HD = 128
STEP = 64
F32 = jnp.float32
BF = jnp.bfloat16


def split(a):
    hi = a.astype(BF)
    return hi, (a - hi.astype(F32)).astype(BF)


def mm(a, b, ca, cb):
    dims = (((ca,), (cb,)), ((), ()))

    def one(x, y):
        return lax.dot_general(x, y, dims, preferred_element_type=F32)

    if isinstance(a, tuple) and isinstance(b, tuple):
        return one(a[0], b[0]) + (one(a[0], b[1]) + one(a[1], b[0]))
    if isinstance(a, tuple):
        return one(a[0], b) + one(a[1], b)
    if isinstance(b, tuple):
        return one(a, b[0]) + one(a, b[1])
    return one(a, b)


def beside(items):
    return tuple(jnp.concatenate([i[p] for i in items], axis=1) for p in range(2))


def cat(items):
    return tuple(jnp.concatenate([i[p] for i in items], axis=0) for p in range(2))


def grids(size):
    return (
        lax.broadcasted_iota(jnp.int32, (size, size), 0),
        lax.broadcasted_iota(jnp.int32, (size, size), 1),
    )


def to_col(row, eye):
    return jnp.sum(jnp.where(eye, row, 0.0), axis=1, keepdims=True)


def strengths(gram, logit_row, eye):
    square = jnp.where(eye, gram, 0.0)
    sig_row = 1.0 / (jnp.sum(square, axis=0, keepdims=True) + 1e-06)
    sig_col = 1.0 / (jnp.sum(square, axis=1, keepdims=True) + 1e-06)
    beta_row = 2.0 * jax.nn.sigmoid(logit_row)
    beta_col = to_col(beta_row, eye)
    return sig_row, sig_col, beta_row, beta_col


def inverses(lows, rows, cols, eye):
    invs = [jnp.where(eye, 1.0, jnp.where((rows ^ cols) == 1, -low, 0.0)) for low in lows]
    size = 2
    while size < rows.shape[0]:
        pair = (rows // size ^ cols // size) == 1
        parts = [split(inv) for inv in invs]
        offs = [split(jnp.where(pair, low, 0.0)) for low in lows]
        mids = [split(mm(off, part, 1, 0)) for off, part in zip(offs, parts)]
        invs = [inv - mm(part, mid, 1, 0) for inv, part, mid in zip(invs, parts, mids)]
        size *= 2
    return invs


def place_of(order_ref, block, per):
    return pl.ds(pl.multiple_of((((block // per) ^ order_ref[0]) * per + block % per) * STEP, STEP), STEP)


def fwd_kernel(per, order_ref, proj_ref, lg_ref, seg_ref, att_ref, pr_ref, qm_ref, x_ref, ft_ref, e_ref, kt_ref, p_ref, s_ref, own_ref):
    length, width = att_ref.shape
    for b in range(length // STEP):
        own_ref[b * STEP : (b + 1) * STEP, :] = proj_ref[place_of(order_ref, b, per), :]
    q_ref, k_ref, v_ref, r_ref = (own_ref.at[:, n * width : (n + 1) * width] for n in range(4))
    blocks = length // width
    rows, cols = grids(width)
    eye = rows == cols
    lows, scales = [], []
    for c in range(blocks):
        r = r_ref[c * width : (c + 1) * width, :]
        gram = mm(r, r, 1, 1)
        sig_row, sig_col, beta_row, beta_col = strengths(gram, lg_ref[0, :, c * width : (c + 1) * width], eye)
        lows.append(jnp.where(rows > cols, gram * (beta_col * sig_col), 0.0))
        scales.append(beta_row * sig_row)
    invs = inverses(lows, rows, cols, eye)

    def chunk(c):
        at = pl.ds(pl.multiple_of(c * width, width), width)
        q, k, r = q_ref[at, :], k_ref[at, :], r_ref[at, :]
        prods = mm(jnp.concatenate([q, k], axis=0), r, 1, 1)
        qr, kr = prods[:width], prods[width : 2 * width]
        inv = invs[c]
        tri = split(inv * scales[c])
        qrl = split(jnp.where(rows >= cols, qr, 0.0))
        kru = split(jnp.where(rows < cols, kr, 0.0))
        ft = mm(kru, tri, 1, 1)
        e = mm(qrl, tri, 1, 0)
        fts, es = split(ft), split(e)
        moved = mm(cat([fts, es, tri]), r, 1, 0)
        s_ref[at, at] = mm(q, k, 1, 1) - mm(qrl, fts, 1, 1)
        kt_ref[0, at, :] = k.astype(F32) - moved[:width]
        qm_ref[0, c, at, :] = q.astype(F32) - moved[width : 2 * width]
        p_ref[0, at, :] = jnp.where(eye, 1.0, 0.0) - mm(r, split(moved[2 * width :]), 0, 0)
        x_ref[0, at, :] = inv
        ft_ref[0, at, :] = ft
        e_ref[0, at, :] = e

    for c in range(blocks):
        chunk(c)

    for j in range(blocks - 1, -1, -1):
        here = pl.ds(j * width, width)
        if j < blocks - 1:
            below = pl.ds((j + 1) * width, length - (j + 1) * width)
            moved = split(qm_ref[0, j, below, :])
            s_ref[below, here] = mm(moved, split(kt_ref[0, here, :]), 1, 1)
            if j:
                qm_ref[0, j - 1, below, :] = mm(moved, split(p_ref[0, here, :]), 1, 0)
        if j:
            qm_ref[0, j - 1, here, :] = qm_ref[0, j, here, :]

    seg_row = seg_ref[0:1, :].astype(F32)
    for i in range(blocks):
        here = pl.ds(i * width, width)
        upto = (i + 1) * width
        seg_col = to_col(seg_row[:, i * width : upto], eye)
        row = lax.broadcasted_iota(jnp.int32, (width, upto), 0) + i * width
        col = lax.broadcasted_iota(jnp.int32, (width, upto), 1)
        ok = (col <= row) & (seg_col == seg_row[:, :upto])
        score = jnp.where(ok, s_ref[here, :upto] * width ** (-0.5), -1e30)
        top = jnp.max(score, axis=1, keepdims=True)
        ex = jnp.exp(score - top)
        prob = ex / jnp.sum(ex, axis=1, keepdims=True)
        pr_ref[0, here, :upto] = prob
        att = mm(split(prob), v_ref[:upto, :], 1, 0).astype(att_ref.dtype)
        for b in range(width // STEP):
            att_ref[place_of(order_ref, i * width // STEP + b, per), :] = att[b * STEP : (b + 1) * STEP]


def attend_fwd(order, proj, logits, seg, quarter):
    length, wide = proj.shape
    heads = wide // (4 * HD)
    blocks = length // HD
    part = pl.BlockSpec((length, 4 * HD), lambda h: (0, h))
    smem = pl.BlockSpec(memory_space=pltpu.SMEM)
    per = pl.BlockSpec((1, length, HD), lambda h: (h, 0, 0))
    st = jax.ShapeDtypeStruct
    return pl.pallas_call(
        functools.partial(fwd_kernel, quarter // STEP),
        grid=(heads,),
        in_specs=[smem, part,
                  pl.BlockSpec((1, 1, length), lambda h: (h, 0, 0)),
                  pl.BlockSpec((1, length), lambda h: (0, 0))],
        out_specs=[pl.BlockSpec((length, HD), lambda h: (0, h)),
                   pl.BlockSpec((1, length, length), lambda h: (h, 0, 0)),
                   pl.BlockSpec((1, blocks, length, HD), lambda h: (h, 0, 0, 0)),
                   per, per, per, per, per],
        out_shape=[st((length, heads * HD), BF), st((heads, length, length), F32),
                   st((heads, blocks, length, HD), F32)] + [st((heads, length, HD), F32)] * 5,
        scratch_shapes=[pltpu.VMEM((length, length), F32), pltpu.VMEM((length, 4 * HD), BF)],
        compiler_params=pltpu.CompilerParams(vmem_limit_bytes=56 << 20, dimension_semantics=("arbitrary",)),
        cost_estimate=pl.CostEstimate(flops=heads * 11 * 10**9, bytes_accessed=heads * 10**7, transcendentals=heads * length * length),
        name="attend_fwd",
    )(order, proj, logits.reshape(heads, 1, length), seg)


def bwd_kernel(per, order_ref, proj_ref, lg_ref, dog_ref, pr_ref, qm_ref, x_ref, ft_ref, e_ref, kt_ref, p_ref,
               dproj_ref, dl_ref, ds_ref, dkt_ref, dqt_ref, dp_ref, own_ref, do_ref, dv_ref):
    length, width = dog_ref.shape
    for b in range(length // STEP):
        rows = slice(b * STEP, (b + 1) * STEP)
        own_ref[rows, :] = proj_ref[place_of(order_ref, b, per), :]
        do_ref[rows, :] = dog_ref[place_of(order_ref, b, per), :]
    q_ref, k_ref, v_ref, r_ref = (own_ref.at[:, n * width : (n + 1) * width] for n in range(4))
    blocks = length // width
    rows, cols = grids(width)
    eye = rows == cols

    for i in range(blocks):
        here = pl.ds(i * width, width)
        upto = (i + 1) * width
        prob = pr_ref[0, here, :upto]
        dprob = mm(do_ref[here, :].astype(BF), v_ref[:upto, :], 1, 1)
        delta = jnp.sum(prob * dprob, axis=1, keepdims=True)
        ds_ref[here, :upto] = prob * (dprob - delta) * width ** (-0.5)
    for j in range(blocks):
        here = pl.ds(j * width, width)
        below = pl.ds(j * width, length - j * width)
        dv_ref[here, :] = mm(pr_ref[0, below, here].astype(BF), do_ref[below, :].astype(BF), 0, 0)

    zero = jnp.zeros((width, width), F32)
    dqt_ref[0:width, :] = zero
    dp_ref[0:width, :] = zero
    last = pl.ds((blocks - 1) * width, width)
    dkt_ref[last, :] = zero
    dp_ref[last, :] = zero
    grad = None
    for j in range(blocks - 1):
        here = pl.ds(j * width, width)
        below = pl.ds((j + 1) * width, length - (j + 1) * width)
        dsj = ds_ref[below, here].astype(BF)
        moved = qm_ref[0, j, below, :].astype(BF)
        dkt_ref[here, :] = mm(dsj, moved, 0, 0)
        fresh = mm(dsj, kt_ref[0, here, :].astype(BF), 1, 0)
        if j:
            old = grad.astype(BF)
            dp_ref[here, :] = mm(moved, old, 0, 0)
            fresh = fresh + mm(old, p_ref[0, here, :].astype(BF), 1, 1)
        dqt_ref[pl.ds((j + 1) * width, width), :] = fresh[:width]
        grad = fresh[width:]

    def chunk(c):
        at = pl.ds(pl.multiple_of(c * width, width), width)
        q, k, r = q_ref[at, :], k_ref[at, :], r_ref[at, :]
        prods = mm(jnp.concatenate([r, q, k], axis=0), r, 1, 1)
        gram, qr, kr = prods[:width], prods[width : 2 * width], prods[2 * width :]
        sig_row, sig_col, beta_row, beta_col = strengths(gram, lg_ref[0, :, at], eye)
        inv = x_ref[0, at, :]
        tri_full = inv * (beta_row * sig_row)
        tri = split(tri_full)
        qrl = split(jnp.where(rows >= cols, qr, 0.0))
        kru = split(jnp.where(rows < cols, kr, 0.0))
        ft, e = split(ft_ref[0, at, :]), split(e_ref[0, at, :])
        dsin = split(ds_ref[at, at])
        dkt_f, dqt_f = dkt_ref[at, :], dqt_ref[at, :]
        dkt, dqt = split(dkt_f), split(dqt_f)
        dp = split(dp_ref[at, :])
        y = split(mm(tri, r, 1, 0))
        dy = split(-mm(r, dp, 1, 0))
        both = mm(cat([dkt, dqt, dy]), r, 1, 1)
        dft = split(-both[:width] - mm(dsin, qrl, 0, 0))
        de = split(-both[width : 2 * width])
        dtri = both[2 * width :] + mm(cat([dft, qrl]), cat([kru, de]), 0, 0)
        dtris = split(dtri)
        dqr = split(jnp.where(rows >= cols, mm(de, tri, 1, 1) - mm(dsin, ft, 1, 0), 0.0))
        dkr = split(jnp.where(rows < cols, mm(dft, tri, 1, 0), 0.0))
        dlow = -mm(split(inv), split(mm(dtris, tri, 1, 1)), 0, 0)
        dlow = jnp.where(rows > cols, dlow, 0.0)
        b_col = beta_col * sig_col
        dgram = split(dlow * b_col)
        db = jnp.sum(dtri * inv, axis=0, keepdims=True)
        db_col = jnp.sum(dlow * gram, axis=1, keepdims=True)
        db = db + jnp.sum(jnp.where(eye, db_col, 0.0), axis=0, keepdims=True)
        dl_ref[0, :, at] = db * sig_row * beta_row * (1.0 - 0.5 * beta_row)
        dst = tuple(jnp.transpose(d) for d in dsin)
        dq = dqt_f + mm(beside([dsin, dqr]), jnp.concatenate([k, r], axis=0), 1, 0)
        dk = dkt_f + mm(beside([dst, dkr]), jnp.concatenate([q, r], axis=0), 1, 0)
        dr = mm(dgram, r, 1, 0) + mm(cat([dqr, dkr, dgram]), jnp.concatenate([q, k, r], axis=0), 0, 0)
        dr = dr - mm(cat([ft, e]), cat([dkt, dqt]), 0, 0) + mm(tri, dy, 0, 0) - mm(y, dp, 1, 1)
        dsig = to_col(db * beta_row, eye)
        dr = dr - (2.0 * dsig * sig_col * sig_col) * r.astype(F32)
        whole = jnp.concatenate([dq, dk, dv_ref[at, :], dr], axis=1).astype(dproj_ref.dtype)
        for b in range(width // STEP):
            dproj_ref[place_of(order_ref, c * width // STEP + b, per), :] = whole[b * STEP : (b + 1) * STEP]

    for c in range(blocks):
        chunk(c)


def attend_bwd(order, proj, logits, saved, grad, quarter):
    length, wide = proj.shape
    heads = wide // (4 * HD)
    blocks = length // HD
    part = pl.BlockSpec((length, 4 * HD), lambda h: (0, h))
    smem = pl.BlockSpec(memory_space=pltpu.SMEM)
    per = pl.BlockSpec((1, length, HD), lambda h: (h, 0, 0))
    col = pl.BlockSpec((length, HD), lambda h: (0, h))
    lrow = pl.BlockSpec((1, 1, length), lambda h: (h, 0, 0))
    st = jax.ShapeDtypeStruct
    scr = pltpu.VMEM((length, HD), F32)
    return pl.pallas_call(
        functools.partial(bwd_kernel, quarter // STEP),
        grid=(heads,),
        in_specs=[smem, part, lrow, col,
                  pl.BlockSpec((1, length, length), lambda h: (h, 0, 0)),
                  pl.BlockSpec((1, blocks, length, HD), lambda h: (h, 0, 0, 0)),
                  per, per, per, per, per],
        out_specs=[part, lrow],
        out_shape=[st((length, wide), BF), st((heads, 1, length), F32)],
        scratch_shapes=[pltpu.VMEM((length, length), F32), scr, scr, scr, pltpu.VMEM((length, 4 * HD), BF), scr, scr],
        compiler_params=pltpu.CompilerParams(vmem_limit_bytes=56 << 20, dimension_semantics=("arbitrary",)),
        cost_estimate=pl.CostEstimate(flops=15 * 10**9, bytes_accessed=10**7, transcendentals=length),
        name="attend_bwd",
    )(order, proj, logits.reshape(heads, 1, length), grad, *saved)


def assemble(pieces, places, widths):
    size, count = pieces[0].shape[0], len(pieces)

    def kernel(place_ref, *refs):
        for n in range(count):
            rows = pl.ds(pl.multiple_of(place_ref[n] * size, size), size)
            start = 0
            for out, width in zip(refs[count:], widths):
                out[rows, :] = refs[n][:, start : start + width]
                start += width

    vmem = pl.BlockSpec(memory_space=pltpu.VMEM)
    return pl.pallas_call(
        kernel,
        in_specs=[pl.BlockSpec(memory_space=pltpu.SMEM)] + [vmem] * count,
        out_specs=[vmem] * len(widths),
        out_shape=[jax.ShapeDtypeStruct((count * size, w), BF) for w in widths],
        compiler_params=pltpu.CompilerParams(vmem_limit_bytes=56 << 20),
        cost_estimate=pl.CostEstimate(flops=0, bytes_accessed=4 * count * size * sum(widths), transcendentals=0),
        name="assemble",
    )(jnp.stack(places), *pieces)


def after(value, *first):
    return lax.optimization_barrier((value,) + first)[0]


class Lane:
    def __init__(self, depth):
        self.depth, self.done = depth, []

    def send(self, value, axis, pairs, *first):
        if len(self.done) >= self.depth:
            first = first + (self.done[-self.depth],)
        if first:
            value = after(value, *first)
        self.done.append(lax.ppermute(value, axis, pairs))
        return self.done[-1]


class Flow:
    def __init__(self, make):
        self.make, self.got, self.sent, self.out = make, None, None, None

    def step(self, *first):
        try:
            self.sent, self.got = self.make.send(first) if self.got is not None else next(self.make)
        except StopIteration as end:
            self.out = end.value
        return self.got

    def finish(self, *first):
        while self.out is None:
            self.step(*first)
        return self.out


def norm_back(values, scale_row, gain, grad_out):
    weighted = grad_out * gain
    grad_gain = jnp.sum(grad_out * values * scale_row, axis=0)
    grad_values = scale_row * weighted - values * scale_row**3 * jnp.mean(
        weighted * values, axis=-1, keepdims=True
    )
    return (grad_gain, grad_values)


def make_body(sizes):
    dp, hid, wid = sizes["dp"], sizes["hid"], sizes["wid"]

    def body(
        hidden_in, cotangent, segments, gain_attn, gain_mlp,
        in_weight, beta_weight, out_weight, gate_weight, up_weight, down_weight,
    ):
        me_dp, me_hid, me_wid = (lax.axis_index(a) for a in ("dp", "hid", "wid"))
        tokens, slice_width = hidden_in.shape
        rows = tokens // wid
        quarter = rows // hid
        heads = in_weight.shape[2] // HD
        shard = in_weight.shape[0]
        lane_x, lane_y, lane_z = Lane(4), Lane(6), Lane(4)

        def dot(a, b, ca, cb, out=F32):
            return lax.dot_general(a, b, (((ca,), (cb,)), ((), ())), preferred_element_type=F32).astype(out)

        def swap(value, bit, *first):
            return lane_x.send(value, "hid", [(i, i ^ bit) for i in range(hid)], *first)

        def to_tokens(array):
            mine = lax.dynamic_index_in_dim(array.reshape(wid, hid, quarter, slice_width), me_hid, 1, keepdims=False)
            return lax.all_to_all(mine.reshape(wid * quarter, slice_width), "wid", split_axis=0, concat_axis=1, tiled=True)

        def gather_hid(own, before=()):
            pieces = {0: own}
            bit = hid // 2
            while bit:
                for k in list(pieces):
                    pieces[k | bit] = swap(after(pieces[k], *before) if before and k else pieces[k], bit)
                bit //= 2
            return [pieces[k] for k in range(hid)]

        def summing_hid(make, first=()):
            keep, bit = list(range(hid)), 1
            send = [k for k in keep if k & bit]
            keep = [k for k in keep if not k & bit]
            sent = make(send).astype(BF)
            got = swap(sent, bit, *first)
            wait = yield sent, got
            total = make(keep) + (after(got, *wait) if wait else got)
            bit *= 2
            while bit < hid:
                low = [n for n, k in enumerate(keep) if not k & bit]
                high = [n for n, k in enumerate(keep) if k & bit]
                part = lambda ns: jnp.concatenate([total[n * quarter : (n + 1) * quarter] for n in ns], axis=0)
                sent = part(high).astype(BF)
                got = swap(sent, bit)
                wait = yield sent, got
                total = part(low) + (after(got, *wait) if wait else got)
                keep = [k for k in keep if not k & bit]
                bit *= 2
            return total

        def sum_hid(make):
            return Flow(summing_hid(make)).finish()

        def reorder(array, axis=0):
            size = array.shape[axis] // hid
            return jnp.concatenate(
                [lax.dynamic_slice_in_dim(array, (me_hid ^ j) * size, size, axis) for j in range(hid)], axis=axis
            )

        def rows_of(array, ks):
            return jnp.concatenate([array[k * quarter : (k + 1) * quarter] for k in ks], axis=0)

        def scattering(make, kept, wid_first=False, first=()):
            def bits(size):
                return [1 << n for n in range(size.bit_length() - 1)]

            def over(axis, lane, parts, bit, first):
                high = [j for j in parts if j & bit]
                sent = jnp.concatenate([parts[j].astype(BF) for j in high], axis=0)
                got = lane.send(sent, axis, [(i, i ^ bit) for i in range(sizes[axis])], *first)
                wait = yield sent, got
                got = after(got, *wait) if wait else got
                low = [j for j in parts if not j & bit]
                size = sent.shape[0] // len(high)
                return {j: parts[j] + got[n * size : (n + 1) * size] for n, j in enumerate(low)}, ()

            parts = {j: make(j) for j in range(dp)}
            kept.append(parts[0])
            if not wid_first:
                for bit in reversed(bits(dp)):
                    parts, first = yield from over("dp", lane_y, parts, bit, first)
            width = parts[0].shape[-1]
            blocks = {j: part.reshape(wid, shard, width) for j, part in parts.items()}
            parts = {
                n: jnp.concatenate([lax.dynamic_index_in_dim(b, me_wid ^ n, 0, keepdims=False) for b in blocks.values()], axis=0)
                for n in range(wid)
            }
            for bit in bits(wid):
                parts, first = yield from over("wid", lane_z, parts, bit, first)
            if wid_first:
                parts = dict(enumerate(jnp.split(parts[0], dp, axis=0)))
                for bit in reversed(bits(dp)):
                    parts, first = yield from over("dp", lane_y, parts, bit, first)
            return parts[0]

        def scatter_grad(left, right, first=(), kept=None):
            kept = [] if kept is None else kept
            return Flow(scattering(lambda by: dot(half(left, by), right, 0, 0), kept, False, first))

        def half(left, by):
            width = left.shape[1] // dp
            return lax.dynamic_slice_in_dim(left, (me_dp ^ by) * width, width, 1)

        def to_widths(own, *first):
            mine = lax.all_to_all(after(own.astype(BF), *first), "wid", split_axis=1, concat_axis=0, tiled=True)
            return mine.reshape(wid, 1, own.shape[0], slice_width)

        def placed(pieces, dtype):
            stacked = reorder(jnp.concatenate([p[:, :, :quarter] for p in pieces], axis=1), axis=1)
            return stacked.reshape(tokens, slice_width).astype(dtype)

        inner, hidden = out_weight.shape[0], gate_weight.shape[1]

        def gather_rows(own):
            return lax.all_gather(own, ("dp", "wid"), axis=0, tiled=True)

        weight_out = gather_rows(out_weight.T)

        hops = list(range(wid))
        hops = [0, 1] + hops[:1:-1] if wid > 2 else hops

        def hop(own, k, *first):
            return lax.ppermute(after(own, *first) if first else own, "wid", [(i, (i + k) % wid) for i in range(wid)])

        def over_dp(piece, *first):
            return [piece] + [lane_y.send(piece, "dp", [(i, (i + by) % dp) for i in range(dp)], *first) for by in range(1, dp)]

        def whole(pieces, widths):
            places = [
                (me_dp + dp - by) % dp * wid + (me_wid + wid - k) % wid for k in hops for by in range(dp)
            ]
            return assemble([p for ps in pieces for p in ps], places, widths)

        token_in = to_tokens(hidden_in)
        width_in = 4 * heads * HD
        columns = [in_weight[:, c, h * HD : (h + 1) * HD] for h in range(heads) for c in range(4)]
        small = [beta_weight, gain_attn[:, None], gain_mlp[:, None], jnp.zeros((shard, HD - heads - 2), BF)]
        own_in = jnp.concatenate(columns + small, axis=1)
        own_late = jnp.concatenate([gate_weight, up_weight, down_weight.T], axis=1)
        along = [own_in] + [hop(own_in, k) for k in hops[1:3]]
        pieces = [over_dp(own_in)]
        tokens_hid = gather_hid(token_in)
        along = along[:1] + [after(a, token_in) for a in along[1:]]
        for k in hops[3:]:
            along.append(hop(own_in, k, *along[1:], pieces[0][-1], tokens_hid[hid // 2]))
        inputs_all = jnp.concatenate(tokens_hid, axis=0).astype(F32)
        pieces += [over_dp(a) for a in along[1:]]
        late_along = [own_late] + [hop(own_late, k, along[-1]) for k in hops[1:3]]
        late = [over_dp(own_late)]
        weight_in, small = whole(pieces, (width_in, HD))
        weight_beta = small[:, :heads]
        gain_one = small[:, heads].astype(F32)
        gain_two = small[:, heads + 1].astype(F32)

        scale_all = lax.rsqrt(jnp.mean(inputs_all * inputs_all, axis=-1, keepdims=True) + 1e-06)
        normed = (inputs_all * scale_all * gain_one).astype(BF)
        projected = dot(after(normed, late[0][-1]), weight_in, 1, 0, BF)
        order = me_hid.reshape(1)
        logits = reorder(dot(normed, weight_beta, 1, 0)).T
        for k in hops[3:]:
            late_along.append(hop(own_late, k, *late_along[1:]))
        late += [over_dp(a) for a in late_along[1:3]]
        token_grad = to_tokens(after(cotangent, projected))
        attended, *saved = attend_fwd(order, after(projected, *late_along[1:3]), logits, segments, quarter)
        attended = after(attended, late[1][-1])

        branch_flow = Flow(summing_hid(lambda ks: dot(rows_of(attended, ks), weight_out, 1, 1)))
        branch_flow.step()
        branch_flow.step(*late_along[3:])
        branch = branch_flow.finish(late[2][-1])
        late += [over_dp(a) for a in late_along[3:]]
        inputs = inputs_all[:quarter]
        scale_one = scale_all[:quarter]
        middle = inputs + branch
        scale_two = lax.rsqrt(jnp.mean(middle * middle, axis=-1, keepdims=True) + 1e-06)
        mixed_own = (middle * scale_two * gain_two).astype(BF)
        mixed = gather_hid(mixed_own)
        mixed = jnp.concatenate(mixed[:-1] + [after(mixed[-1], late[-1][-1])], axis=0)
        grad_all = jnp.concatenate(gather_hid(after(token_grad, mixed_own)), axis=0)
        weight_mlp, weight_down = whole(late, (2 * hidden, hidden))
        gate_up = dot(mixed, weight_mlp, 1, 0)
        gate, upward = gate_up[:, :hidden], gate_up[:, hidden:]
        sigmoid_gate = jax.nn.sigmoid(gate)
        silu_gate = gate * sigmoid_gate
        product = (silu_gate * upward).astype(BF)
        def scatter_plain(full):
            return lax.psum_scatter(full, ("dp", "wid"), scatter_dimension=0, tiled=True).astype(F32)

        down_full = dot(grad_all, product, 0, 0, BF)
        grad_down = scatter_plain(down_full)
        grad_product = dot(grad_all, weight_down, 1, 0)
        grad_gate_pre = grad_product * upward * sigmoid_gate * (1.0 + gate * (1.0 - sigmoid_gate))
        grad_gate_pre, grad_up_pre = grad_gate_pre.astype(BF), (grad_product * silu_gate).astype(BF)
        kept = [down_full]
        gate_flow, up_flow = (scatter_grad(mixed, g, kept=kept) for g in (grad_gate_pre, grad_up_pre))
        grad_pre = jnp.concatenate([grad_gate_pre, grad_up_pre], axis=1)
        mixed_flow = Flow(summing_hid(lambda ks: dot(rows_of(grad_pre, ks), weight_mlp, 1, 1)))
        mixed_flow.step()
        gate_flow.step()
        mixed_flow.step()
        feed_flow = Flow(summing_hid(lambda ks: dot(rows_of(product, ks), weight_down, 1, 1)))
        feed_flow.step()
        grad_mixed = mixed_flow.finish()
        up_flow.step()
        grad_gain_two, grad_middle = norm_back(middle, scale_two, gain_two, grad_mixed)
        grad_middle = grad_middle + token_grad.astype(F32)
        quarters = gather_hid(grad_middle.astype(BF), kept)
        grad_branch = after(jnp.concatenate(quarters, axis=0), gate_flow.got, *kept)
        grad_attended = dot(grad_branch, weight_out, 1, 0)
        gate_flow.step(grad_branch)
        feed_flow.step(grad_branch)

        grad_proj, grad_logit = attend_bwd(order, projected, logits, saved, grad_attended, quarter)
        grad_proj = after(grad_proj, up_flow.got, feed_flow.got)
        grad_logit = grad_logit[:, 0, :]
        logit_parts = jnp.concatenate(split(reorder(grad_logit, axis=1)), axis=0)
        beta_twice = jnp.concatenate([weight_beta, weight_beta], axis=1)

        def back(ks):
            lower = jnp.concatenate([logit_parts[:, k * quarter : (k + 1) * quarter] for k in ks], axis=1)
            return dot(rows_of(grad_proj, ks), weight_in, 1, 1) + dot(lower, beta_twice, 0, 1)

        back_flow = Flow(summing_hid(back))
        back_flow.step()
        begun = back_flow.sent
        in_flow = scatter_grad(normed, after(grad_proj, begun))
        in_flow.step()
        up_flow.step(begun)
        feed_widths = to_widths(middle + feed_flow.finish(begun))
        back_flow.step()
        handed = back_flow.sent
        grad_normed = back_flow.finish()
        gate_flow.step(handed)
        grad_gain_one, grad_inputs = norm_back(inputs, scale_one, gain_one, grad_normed)
        grad_beta = dot(after(logit_parts, handed), normed, 1, 0)
        grad_beta = grad_beta[:heads] + grad_beta[heads:]
        vectors = jnp.concatenate([grad_gain_one[None], grad_gain_two[None], grad_beta], axis=0)
        count = vectors.shape[0]
        vectors = vectors.reshape(count, dp, wid, shard).transpose(0, 2, 1, 3).reshape(count, wid * dp * shard)
        extra = jnp.concatenate(split(vectors), axis=0)
        extra = jnp.pad(extra, ((0, -(2 * count) % 16), (0, 0)))
        ended = jnp.concatenate([(grad_inputs + grad_middle).astype(BF), extra], axis=0)
        grad_widths = to_widths(ended)
        in_flow.step(ended)
        up_flow.step(grad_widths)
        grad_out = scatter_plain(dot(grad_branch, after(attended, handed), 0, 0, BF))
        out_pieces = gather_hid(after(feed_widths, ended))
        in_pieces = gather_hid(grad_widths)
        arrived = in_pieces[hid // 2]
        in_flow.step(grad_widths)
        passed = in_flow.sent
        grad_gate, grad_up = gate_flow.finish(arrived), up_flow.finish(passed)

        def row_sums(piece):
            both = jnp.sum(piece[:, 0, quarter : quarter + 2 * count].astype(F32), axis=0)
            return (both[:count] + both[count:]).reshape(count, dp, shard)

        sums = [row_sums(p) for p in in_pieces]
        gains = functools.reduce(jnp.add, [one[:2] for one in sums])
        sums = jnp.concatenate([gains, sums[0][2:]], axis=0)
        vectors = lax.dynamic_index_in_dim(sums, me_dp, 1, keepdims=False)
        for by in range(1, dp):
            theirs = lax.dynamic_index_in_dim(sums, (me_dp + by) % dp, 1, keepdims=False)
            vectors = vectors + lax.ppermute(theirs, "dp", [(i, (i + by) % dp) for i in range(dp)])
        in_pieces = [after(p, passed) for p in in_pieces]
        output, grad_input = placed(out_pieces, BF), placed(in_pieces, F32)
        grad_in = in_flow.finish().reshape(shard, heads, 4, HD).transpose(0, 2, 1, 3).reshape(shard, 4, heads * HD)

        return (
            output, grad_input, vectors[0], vectors[1], grad_in, vectors[2:].T, grad_out.T,
            grad_gate, grad_up, grad_down.T,
        )

    return body


def solution(mesh):
    by_rows, by_cols = P(("dp", "wid"), "hid"), P("hid", ("dp", "wid"))
    both = P(("dp", "wid"))
    deep = P(("dp", "wid"), None, "hid")
    wide = P("dp", "wid")
    return jax.shard_map(
        make_body(dict(mesh.shape)),
        mesh=mesh,
        in_specs=(wide, wide, P(("dp", "wid"), None), both, both, deep, by_rows, by_cols, by_rows, by_rows, by_cols),
        out_specs=(wide, wide, both, both, deep, by_rows, by_cols, by_rows, by_rows, by_cols),
        check_vma=False,
    )
```

```python
import functools
import jax, jax.numpy as jnp
from jax import lax
from jax.experimental import pallas as pl
from jax.experimental.pallas import tpu as pltpu
from jax.sharding import PartitionSpec as P

HD = 128
STEP = 64
F32 = jnp.float32
BF = jnp.bfloat16


def split(a):
    hi = a.astype(BF)
    return hi, (a - hi.astype(F32)).astype(BF)


def mm(a, b, ca, cb):
    dims = (((ca,), (cb,)), ((), ()))

    def one(x, y):
        return lax.dot_general(x, y, dims, preferred_element_type=F32)

    if isinstance(a, tuple) and isinstance(b, tuple):
        return one(a[0], b[0]) + (one(a[0], b[1]) + one(a[1], b[0]))
    if isinstance(a, tuple):
        return one(a[0], b) + one(a[1], b)
    if isinstance(b, tuple):
        return one(a, b[0]) + one(a, b[1])
    return one(a, b)


def beside(items):
    return tuple(jnp.concatenate([i[p] for i in items], axis=1) for p in range(2))


def cat(items):
    return tuple(jnp.concatenate([i[p] for i in items], axis=0) for p in range(2))


def grids(size):
    return (
        lax.broadcasted_iota(jnp.int32, (size, size), 0),
        lax.broadcasted_iota(jnp.int32, (size, size), 1),
    )


def to_col(row, eye):
    return jnp.sum(jnp.where(eye, row, 0.0), axis=1, keepdims=True)


def strengths(gram, logit_row, eye):
    square = jnp.where(eye, gram, 0.0)
    sig_row = 1.0 / (jnp.sum(square, axis=0, keepdims=True) + 1e-06)
    sig_col = 1.0 / (jnp.sum(square, axis=1, keepdims=True) + 1e-06)
    beta_row = 2.0 * jax.nn.sigmoid(logit_row)
    beta_col = to_col(beta_row, eye)
    return sig_row, sig_col, beta_row, beta_col


def inverses(lows, rows, cols, eye):
    invs = [jnp.where(eye, 1.0, jnp.where((rows ^ cols) == 1, -low, 0.0)) for low in lows]
    size = 2
    while size < rows.shape[0]:
        pair = (rows // size ^ cols // size) == 1
        parts = [split(inv) for inv in invs]
        offs = [split(jnp.where(pair, low, 0.0)) for low in lows]
        mids = [split(mm(off, part, 1, 0)) for off, part in zip(offs, parts)]
        invs = [inv - mm(part, mid, 1, 0) for inv, part, mid in zip(invs, parts, mids)]
        size *= 2
    return invs


def place_of(order_ref, block, per):
    return pl.ds(pl.multiple_of((((block // per) ^ order_ref[0]) * per + block % per) * STEP, STEP), STEP)


def fwd_kernel(per, order_ref, proj_ref, lg_ref, seg_ref, att_ref, pr_ref, qm_ref, x_ref, ft_ref, e_ref, kt_ref, p_ref, s_ref, own_ref):
    length, width = att_ref.shape
    for b in range(length // STEP):
        own_ref[b * STEP : (b + 1) * STEP, :] = proj_ref[place_of(order_ref, b, per), :]
    q_ref, k_ref, v_ref, r_ref = (own_ref.at[:, n * width : (n + 1) * width] for n in range(4))
    blocks = length // width
    rows, cols = grids(width)
    eye = rows == cols
    lows, scales = [], []
    for c in range(blocks):
        r = r_ref[c * width : (c + 1) * width, :]
        gram = mm(r, r, 1, 1)
        sig_row, sig_col, beta_row, beta_col = strengths(gram, lg_ref[0, :, c * width : (c + 1) * width], eye)
        lows.append(jnp.where(rows > cols, gram * (beta_col * sig_col), 0.0))
        scales.append(beta_row * sig_row)
    invs = inverses(lows, rows, cols, eye)

    def chunk(c):
        at = pl.ds(pl.multiple_of(c * width, width), width)
        q, k, r = q_ref[at, :], k_ref[at, :], r_ref[at, :]
        prods = mm(jnp.concatenate([q, k], axis=0), r, 1, 1)
        qr, kr = prods[:width], prods[width : 2 * width]
        inv = invs[c]
        tri = split(inv * scales[c])
        qrl = split(jnp.where(rows >= cols, qr, 0.0))
        kru = split(jnp.where(rows < cols, kr, 0.0))
        ft = mm(kru, tri, 1, 1)
        e = mm(qrl, tri, 1, 0)
        fts, es = split(ft), split(e)
        moved = mm(cat([fts, es, tri]), r, 1, 0)
        s_ref[at, at] = mm(q, k, 1, 1) - mm(qrl, fts, 1, 1)
        kt_ref[0, at, :] = k.astype(F32) - moved[:width]
        qm_ref[0, c, at, :] = q.astype(F32) - moved[width : 2 * width]
        p_ref[0, at, :] = jnp.where(eye, 1.0, 0.0) - mm(r, split(moved[2 * width :]), 0, 0)
        x_ref[0, at, :] = inv
        ft_ref[0, at, :] = ft
        e_ref[0, at, :] = e

    for c in range(blocks):
        chunk(c)

    for j in range(blocks - 1, -1, -1):
        here = pl.ds(j * width, width)
        if j < blocks - 1:
            below = pl.ds((j + 1) * width, length - (j + 1) * width)
            moved = split(qm_ref[0, j, below, :])
            s_ref[below, here] = mm(moved, split(kt_ref[0, here, :]), 1, 1)
            if j:
                qm_ref[0, j - 1, below, :] = mm(moved, split(p_ref[0, here, :]), 1, 0)
        if j:
            qm_ref[0, j - 1, here, :] = qm_ref[0, j, here, :]

    seg_row = seg_ref[0:1, :].astype(F32)
    for i in range(blocks):
        here = pl.ds(i * width, width)
        upto = (i + 1) * width
        seg_col = to_col(seg_row[:, i * width : upto], eye)
        row = lax.broadcasted_iota(jnp.int32, (width, upto), 0) + i * width
        col = lax.broadcasted_iota(jnp.int32, (width, upto), 1)
        ok = (col <= row) & (seg_col == seg_row[:, :upto])
        score = jnp.where(ok, s_ref[here, :upto] * width ** (-0.5), -1e30)
        top = jnp.max(score, axis=1, keepdims=True)
        ex = jnp.exp(score - top)
        prob = ex / jnp.sum(ex, axis=1, keepdims=True)
        pr_ref[0, here, :upto] = prob
        att = mm(prob.astype(BF), v_ref[:upto, :], 1, 0).astype(att_ref.dtype)
        for b in range(width // STEP):
            att_ref[place_of(order_ref, i * width // STEP + b, per), :] = att[b * STEP : (b + 1) * STEP]


def attend_fwd(order, proj, logits, seg, quarter):
    length, wide = proj.shape
    heads = wide // (4 * HD)
    blocks = length // HD
    part = pl.BlockSpec((length, 4 * HD), lambda h: (0, h))
    smem = pl.BlockSpec(memory_space=pltpu.SMEM)
    per = pl.BlockSpec((1, length, HD), lambda h: (h, 0, 0))
    st = jax.ShapeDtypeStruct
    return pl.pallas_call(
        functools.partial(fwd_kernel, quarter // STEP),
        grid=(heads,),
        in_specs=[smem, part,
                  pl.BlockSpec((1, 1, length), lambda h: (h, 0, 0)),
                  pl.BlockSpec((1, length), lambda h: (0, 0))],
        out_specs=[pl.BlockSpec((length, HD), lambda h: (0, h)),
                   pl.BlockSpec((1, length, length), lambda h: (h, 0, 0)),
                   pl.BlockSpec((1, blocks, length, HD), lambda h: (h, 0, 0, 0)),
                   per, per, per, per, per],
        out_shape=[st((length, heads * HD), BF), st((heads, length, length), F32),
                   st((heads, blocks, length, HD), F32)] + [st((heads, length, HD), F32)] * 5,
        scratch_shapes=[pltpu.VMEM((length, length), F32), pltpu.VMEM((length, 4 * HD), BF)],
        compiler_params=pltpu.CompilerParams(vmem_limit_bytes=56 << 20, dimension_semantics=("arbitrary",)),
        cost_estimate=pl.CostEstimate(flops=heads * 11 * 10**9, bytes_accessed=heads * 10**7, transcendentals=heads * length * length),
        name="attend_fwd",
    )(order, proj, logits.reshape(heads, 1, length), seg)


def bwd_kernel(per, order_ref, proj_ref, lg_ref, dog_ref, pr_ref, qm_ref, x_ref, ft_ref, e_ref, kt_ref, p_ref,
               dproj_ref, dl_ref, ds_ref, dkt_ref, dqt_ref, dp_ref, own_ref, do_ref, dv_ref):
    length, width = dog_ref.shape
    for b in range(length // STEP):
        rows = slice(b * STEP, (b + 1) * STEP)
        own_ref[rows, :] = proj_ref[place_of(order_ref, b, per), :]
        do_ref[rows, :] = dog_ref[place_of(order_ref, b, per), :]
    q_ref, k_ref, v_ref, r_ref = (own_ref.at[:, n * width : (n + 1) * width] for n in range(4))
    blocks = length // width
    rows, cols = grids(width)
    eye = rows == cols

    for i in range(blocks):
        here = pl.ds(i * width, width)
        upto = (i + 1) * width
        prob = pr_ref[0, here, :upto]
        dprob = mm(do_ref[here, :].astype(BF), v_ref[:upto, :], 1, 1)
        delta = jnp.sum(prob * dprob, axis=1, keepdims=True)
        ds_ref[here, :upto] = prob * (dprob - delta) * width ** (-0.5)
    for j in range(blocks):
        here = pl.ds(j * width, width)
        below = pl.ds(j * width, length - j * width)
        dv_ref[here, :] = mm(pr_ref[0, below, here].astype(BF), do_ref[below, :].astype(BF), 0, 0)

    zero = jnp.zeros((width, width), F32)
    dqt_ref[0:width, :] = zero
    dp_ref[0:width, :] = zero
    last = pl.ds((blocks - 1) * width, width)
    dkt_ref[last, :] = zero
    dp_ref[last, :] = zero
    grad = None
    for j in range(blocks - 1):
        here = pl.ds(j * width, width)
        below = pl.ds((j + 1) * width, length - (j + 1) * width)
        dsj = ds_ref[below, here].astype(BF)
        moved = qm_ref[0, j, below, :].astype(BF)
        dkt_ref[here, :] = mm(dsj, moved, 0, 0)
        fresh = mm(dsj, kt_ref[0, here, :].astype(BF), 1, 0)
        if j:
            old = grad.astype(BF)
            dp_ref[here, :] = mm(moved, old, 0, 0)
            fresh = fresh + mm(old, p_ref[0, here, :].astype(BF), 1, 1)
        dqt_ref[pl.ds((j + 1) * width, width), :] = fresh[:width]
        grad = fresh[width:]

    def chunk(c):
        at = pl.ds(pl.multiple_of(c * width, width), width)
        q, k, r = q_ref[at, :], k_ref[at, :], r_ref[at, :]
        prods = mm(jnp.concatenate([r, q, k], axis=0), r, 1, 1)
        gram, qr, kr = prods[:width], prods[width : 2 * width], prods[2 * width :]
        sig_row, sig_col, beta_row, beta_col = strengths(gram, lg_ref[0, :, at], eye)
        inv = x_ref[0, at, :]
        tri_full = inv * (beta_row * sig_row)
        tri = split(tri_full)
        qrl = split(jnp.where(rows >= cols, qr, 0.0))
        kru = split(jnp.where(rows < cols, kr, 0.0))
        ft, e = split(ft_ref[0, at, :]), split(e_ref[0, at, :])
        dsin = split(ds_ref[at, at])
        dkt_f, dqt_f = dkt_ref[at, :], dqt_ref[at, :]
        dkt, dqt = split(dkt_f), split(dqt_f)
        dp = split(dp_ref[at, :])
        y = split(mm(tri, r, 1, 0))
        dy = split(-mm(r, dp, 1, 0))
        both = mm(cat([dkt, dqt, dy]), r, 1, 1)
        dft = split(-both[:width] - mm(dsin, qrl, 0, 0))
        de = split(-both[width : 2 * width])
        dtri = both[2 * width :] + mm(cat([dft, qrl]), cat([kru, de]), 0, 0)
        dtris = split(dtri)
        dqr = split(jnp.where(rows >= cols, mm(de, tri, 1, 1) - mm(dsin, ft, 1, 0), 0.0))
        dkr = split(jnp.where(rows < cols, mm(dft, tri, 1, 0), 0.0))
        dlow = -mm(split(inv), split(mm(dtris, tri, 1, 1)), 0, 0)
        dlow = jnp.where(rows > cols, dlow, 0.0)
        b_col = beta_col * sig_col
        dgram = split(dlow * b_col)
        db = jnp.sum(dtri * inv, axis=0, keepdims=True)
        db_col = jnp.sum(dlow * gram, axis=1, keepdims=True)
        db = db + jnp.sum(jnp.where(eye, db_col, 0.0), axis=0, keepdims=True)
        dl_ref[0, :, at] = db * sig_row * beta_row * (1.0 - 0.5 * beta_row)
        dst = tuple(jnp.transpose(d) for d in dsin)
        dq = dqt_f + mm(beside([dsin, dqr]), jnp.concatenate([k, r], axis=0), 1, 0)
        dk = dkt_f + mm(beside([dst, dkr]), jnp.concatenate([q, r], axis=0), 1, 0)
        dr = mm(dgram, r, 1, 0) + mm(cat([dqr, dkr, dgram]), jnp.concatenate([q, k, r], axis=0), 0, 0)
        dr = dr - mm(cat([ft, e]), cat([dkt, dqt]), 0, 0) + mm(tri, dy, 0, 0) - mm(y, dp, 1, 1)
        dsig = to_col(db * beta_row, eye)
        dr = dr - (2.0 * dsig * sig_col * sig_col) * r.astype(F32)
        whole = jnp.concatenate([dq, dk, dv_ref[at, :], dr], axis=1).astype(dproj_ref.dtype)
        for b in range(width // STEP):
            dproj_ref[place_of(order_ref, c * width // STEP + b, per), :] = whole[b * STEP : (b + 1) * STEP]

    for c in range(blocks):
        chunk(c)


def attend_bwd(order, proj, logits, saved, grad, quarter):
    length, wide = proj.shape
    heads = wide // (4 * HD)
    blocks = length // HD
    part = pl.BlockSpec((length, 4 * HD), lambda h: (0, h))
    smem = pl.BlockSpec(memory_space=pltpu.SMEM)
    per = pl.BlockSpec((1, length, HD), lambda h: (h, 0, 0))
    col = pl.BlockSpec((length, HD), lambda h: (0, h))
    lrow = pl.BlockSpec((1, 1, length), lambda h: (h, 0, 0))
    st = jax.ShapeDtypeStruct
    scr = pltpu.VMEM((length, HD), F32)
    return pl.pallas_call(
        functools.partial(bwd_kernel, quarter // STEP),
        grid=(heads,),
        in_specs=[smem, part, lrow, col,
                  pl.BlockSpec((1, length, length), lambda h: (h, 0, 0)),
                  pl.BlockSpec((1, blocks, length, HD), lambda h: (h, 0, 0, 0)),
                  per, per, per, per, per],
        out_specs=[part, lrow],
        out_shape=[st((length, wide), BF), st((heads, 1, length), F32)],
        scratch_shapes=[pltpu.VMEM((length, length), F32), scr, scr, scr, pltpu.VMEM((length, 4 * HD), BF), scr, scr],
        compiler_params=pltpu.CompilerParams(vmem_limit_bytes=56 << 20, dimension_semantics=("arbitrary",)),
        cost_estimate=pl.CostEstimate(flops=15 * 10**9, bytes_accessed=10**7, transcendentals=length),
        name="attend_bwd",
    )(order, proj, logits.reshape(heads, 1, length), grad, *saved)


def assemble(pieces, places, widths):
    size, count = pieces[0].shape[0], len(pieces)

    def kernel(place_ref, *refs):
        for n in range(count):
            rows = pl.ds(pl.multiple_of(place_ref[n] * size, size), size)
            start = 0
            for out, width in zip(refs[count:], widths):
                out[rows, :] = refs[n][:, start : start + width]
                start += width

    vmem = pl.BlockSpec(memory_space=pltpu.VMEM)
    return pl.pallas_call(
        kernel,
        in_specs=[pl.BlockSpec(memory_space=pltpu.SMEM)] + [vmem] * count,
        out_specs=[vmem] * len(widths),
        out_shape=[jax.ShapeDtypeStruct((count * size, w), BF) for w in widths],
        compiler_params=pltpu.CompilerParams(vmem_limit_bytes=56 << 20),
        cost_estimate=pl.CostEstimate(flops=0, bytes_accessed=4 * count * size * sum(widths), transcendentals=0),
        name="assemble",
    )(jnp.stack(places), *pieces)


def after(value, *first):
    return lax.optimization_barrier((value,) + first)[0]


class Lane:
    def __init__(self, depth):
        self.depth, self.done = depth, []

    def send(self, value, axis, pairs, *first):
        if len(self.done) >= self.depth:
            first = first + (self.done[-self.depth],)
        if first:
            value = after(value, *first)
        self.done.append(lax.ppermute(value, axis, pairs))
        return self.done[-1]


class Flow:
    def __init__(self, make):
        self.make, self.got, self.sent, self.out = make, None, None, None

    def step(self, *first):
        try:
            self.sent, self.got = self.make.send(first) if self.got is not None else next(self.make)
        except StopIteration as end:
            self.out = end.value
        return self.got

    def finish(self, *first):
        while self.out is None:
            self.step(*first)
        return self.out


def norm_back(values, scale_row, gain, grad_out):
    weighted = grad_out * gain
    grad_gain = jnp.sum(grad_out * values * scale_row, axis=0)
    grad_values = scale_row * weighted - values * scale_row**3 * jnp.mean(
        weighted * values, axis=-1, keepdims=True
    )
    return (grad_gain, grad_values)


def make_body(sizes):
    dp, hid, wid = sizes["dp"], sizes["hid"], sizes["wid"]

    def body(
        hidden_in, cotangent, segments, gain_attn, gain_mlp,
        in_weight, beta_weight, out_weight, gate_weight, up_weight, down_weight,
    ):
        me_dp, me_hid, me_wid = (lax.axis_index(a) for a in ("dp", "hid", "wid"))
        tokens, slice_width = hidden_in.shape
        rows = tokens // wid
        quarter = rows // hid
        heads = in_weight.shape[2] // HD
        shard = in_weight.shape[0]
        lane_x, lane_y, lane_z = Lane(4), Lane(6), Lane(4)

        def dot(a, b, ca, cb, out=F32):
            return lax.dot_general(a, b, (((ca,), (cb,)), ((), ())), preferred_element_type=F32).astype(out)

        def swap(value, bit, *first):
            return lane_x.send(value, "hid", [(i, i ^ bit) for i in range(hid)], *first)

        def to_tokens(array):
            mine = lax.dynamic_index_in_dim(array.reshape(wid, hid, quarter, slice_width), me_hid, 1, keepdims=False)
            return lax.all_to_all(mine.reshape(wid * quarter, slice_width), "wid", split_axis=0, concat_axis=1, tiled=True)

        def gather_hid(own, before=()):
            pieces = {0: own}
            bit = hid // 2
            while bit:
                for k in list(pieces):
                    pieces[k | bit] = swap(after(pieces[k], *before) if before and k else pieces[k], bit)
                bit //= 2
            return [pieces[k] for k in range(hid)]

        def summing_hid(make, first=()):
            keep, bit = list(range(hid)), 1
            send = [k for k in keep if k & bit]
            keep = [k for k in keep if not k & bit]
            sent = make(send).astype(BF)
            got = swap(sent, bit, *first)
            wait = yield sent, got
            total = make(keep) + (after(got, *wait) if wait else got)
            bit *= 2
            while bit < hid:
                low = [n for n, k in enumerate(keep) if not k & bit]
                high = [n for n, k in enumerate(keep) if k & bit]
                part = lambda ns: jnp.concatenate([total[n * quarter : (n + 1) * quarter] for n in ns], axis=0)
                sent = part(high).astype(BF)
                got = swap(sent, bit)
                wait = yield sent, got
                total = part(low) + (after(got, *wait) if wait else got)
                keep = [k for k in keep if not k & bit]
                bit *= 2
            return total

        def sum_hid(make):
            return Flow(summing_hid(make)).finish()

        def reorder(array, axis=0):
            size = array.shape[axis] // hid
            return jnp.concatenate(
                [lax.dynamic_slice_in_dim(array, (me_hid ^ j) * size, size, axis) for j in range(hid)], axis=axis
            )

        def rows_of(array, ks):
            return jnp.concatenate([array[k * quarter : (k + 1) * quarter] for k in ks], axis=0)

        def scattering(make, kept, wid_first=False, first=()):
            def bits(size):
                return [1 << n for n in range(size.bit_length() - 1)]

            def over(axis, lane, parts, bit, first):
                high = [j for j in parts if j & bit]
                sent = jnp.concatenate([parts[j].astype(BF) for j in high], axis=0)
                got = lane.send(sent, axis, [(i, i ^ bit) for i in range(sizes[axis])], *first)
                wait = yield sent, got
                got = after(got, *wait) if wait else got
                low = [j for j in parts if not j & bit]
                size = sent.shape[0] // len(high)
                return {j: parts[j] + got[n * size : (n + 1) * size] for n, j in enumerate(low)}, ()

            parts = {j: make(j) for j in range(dp)}
            kept.append(parts[0])
            if not wid_first:
                for bit in reversed(bits(dp)):
                    parts, first = yield from over("dp", lane_y, parts, bit, first)
            width = parts[0].shape[-1]
            blocks = {j: part.reshape(wid, shard, width) for j, part in parts.items()}
            parts = {
                n: jnp.concatenate([lax.dynamic_index_in_dim(b, me_wid ^ n, 0, keepdims=False) for b in blocks.values()], axis=0)
                for n in range(wid)
            }
            for bit in bits(wid):
                parts, first = yield from over("wid", lane_z, parts, bit, first)
            if wid_first:
                parts = dict(enumerate(jnp.split(parts[0], dp, axis=0)))
                for bit in reversed(bits(dp)):
                    parts, first = yield from over("dp", lane_y, parts, bit, first)
            return parts[0]

        def scatter_grad(left, right, first=(), kept=None):
            kept = [] if kept is None else kept
            return Flow(scattering(lambda by: dot(half(left, by), right, 0, 0), kept, False, first))

        def half(left, by):
            width = left.shape[1] // dp
            return lax.dynamic_slice_in_dim(left, (me_dp ^ by) * width, width, 1)

        def to_widths(own, *first):
            mine = lax.all_to_all(after(own.astype(BF), *first), "wid", split_axis=1, concat_axis=0, tiled=True)
            return mine.reshape(wid, 1, own.shape[0], slice_width)

        def placed(pieces, dtype):
            stacked = reorder(jnp.concatenate([p[:, :, :quarter] for p in pieces], axis=1), axis=1)
            return stacked.reshape(tokens, slice_width).astype(dtype)

        inner, hidden = out_weight.shape[0], gate_weight.shape[1]

        def gather_rows(own):
            return lax.all_gather(own, ("dp", "wid"), axis=0, tiled=True)

        weight_out = gather_rows(out_weight.T)

        hops = list(range(wid))
        hops = [0, 1] + hops[:1:-1] if wid > 2 else hops

        def hop(own, k, *first):
            return lax.ppermute(after(own, *first) if first else own, "wid", [(i, (i + k) % wid) for i in range(wid)])

        def over_dp(piece, *first):
            return [piece] + [lane_y.send(piece, "dp", [(i, (i + by) % dp) for i in range(dp)], *first) for by in range(1, dp)]

        def whole(pieces, widths):
            places = [
                (me_dp + dp - by) % dp * wid + (me_wid + wid - k) % wid for k in hops for by in range(dp)
            ]
            return assemble([p for ps in pieces for p in ps], places, widths)

        token_in = to_tokens(hidden_in)
        width_in = 4 * heads * HD
        columns = [in_weight[:, c, h * HD : (h + 1) * HD] for h in range(heads) for c in range(4)]
        small = [beta_weight, gain_attn[:, None], gain_mlp[:, None], jnp.zeros((shard, HD - heads - 2), BF)]
        own_in = jnp.concatenate(columns + small, axis=1)
        own_late = jnp.concatenate([gate_weight, up_weight, down_weight.T], axis=1)
        along = [own_in] + [hop(own_in, k) for k in hops[1:3]]
        pieces = [over_dp(own_in)]
        tokens_hid = gather_hid(token_in)
        along = along[:1] + [after(a, token_in) for a in along[1:]]
        for k in hops[3:]:
            along.append(hop(own_in, k, *along[1:], pieces[0][-1], tokens_hid[hid // 2]))
        inputs_all = jnp.concatenate(tokens_hid, axis=0).astype(F32)
        pieces += [over_dp(a) for a in along[1:]]
        late_along = [own_late] + [hop(own_late, k, along[-1]) for k in hops[1:3]]
        late = [over_dp(own_late)]
        weight_in, small = whole(pieces, (width_in, HD))
        weight_beta = small[:, :heads]
        gain_one = small[:, heads].astype(F32)
        gain_two = small[:, heads + 1].astype(F32)

        scale_all = lax.rsqrt(jnp.mean(inputs_all * inputs_all, axis=-1, keepdims=True) + 1e-06)
        normed = (inputs_all * scale_all * gain_one).astype(BF)
        projected = dot(after(normed, late[0][-1]), weight_in, 1, 0, BF)
        order = me_hid.reshape(1)
        logits = reorder(dot(normed, weight_beta, 1, 0)).T
        for k in hops[3:]:
            late_along.append(hop(own_late, k, *late_along[1:]))
        late += [over_dp(a) for a in late_along[1:3]]
        token_grad = to_tokens(after(cotangent, projected))
        attended, *saved = attend_fwd(order, after(projected, *late_along[1:3]), logits, segments, quarter)
        attended = after(attended, late[1][-1])

        branch_flow = Flow(summing_hid(lambda ks: dot(rows_of(attended, ks), weight_out, 1, 1)))
        branch_flow.step()
        branch_flow.step(*late_along[3:])
        branch = branch_flow.finish(late[2][-1])
        late += [over_dp(a) for a in late_along[3:]]
        inputs = inputs_all[:quarter]
        scale_one = scale_all[:quarter]
        middle = inputs + branch
        scale_two = lax.rsqrt(jnp.mean(middle * middle, axis=-1, keepdims=True) + 1e-06)
        mixed_own = (middle * scale_two * gain_two).astype(BF)
        mixed = gather_hid(mixed_own)
        mixed = jnp.concatenate(mixed[:-1] + [after(mixed[-1], late[-1][-1])], axis=0)
        grad_all = jnp.concatenate(gather_hid(after(token_grad, mixed_own)), axis=0)
        weight_mlp, weight_down = whole(late, (2 * hidden, hidden))
        gate_up = dot(mixed, weight_mlp, 1, 0)
        gate, upward = gate_up[:, :hidden], gate_up[:, hidden:]
        sigmoid_gate = jax.nn.sigmoid(gate)
        silu_gate = gate * sigmoid_gate
        product = (silu_gate * upward).astype(BF)
        def scatter_plain(full):
            return lax.psum_scatter(full, ("dp", "wid"), scatter_dimension=0, tiled=True).astype(F32)

        down_full = dot(grad_all, product, 0, 0, BF)
        grad_down = scatter_plain(down_full)
        grad_product = dot(grad_all, weight_down, 1, 0)
        grad_gate_pre = grad_product * upward * sigmoid_gate * (1.0 + gate * (1.0 - sigmoid_gate))
        grad_gate_pre, grad_up_pre = grad_gate_pre.astype(BF), (grad_product * silu_gate).astype(BF)
        kept = [down_full]
        gate_flow, up_flow = (scatter_grad(mixed, g, kept=kept) for g in (grad_gate_pre, grad_up_pre))
        grad_pre = jnp.concatenate([grad_gate_pre, grad_up_pre], axis=1)
        mixed_flow = Flow(summing_hid(lambda ks: dot(rows_of(grad_pre, ks), weight_mlp, 1, 1)))
        mixed_flow.step()
        gate_flow.step()
        mixed_flow.step()
        feed_flow = Flow(summing_hid(lambda ks: dot(rows_of(product, ks), weight_down, 1, 1)))
        feed_flow.step()
        grad_mixed = mixed_flow.finish()
        up_flow.step()
        grad_gain_two, grad_middle = norm_back(middle, scale_two, gain_two, grad_mixed)
        grad_middle = grad_middle + token_grad.astype(F32)
        quarters = gather_hid(grad_middle.astype(BF), kept)
        grad_branch = after(jnp.concatenate(quarters, axis=0), gate_flow.got, *kept)
        grad_attended = dot(grad_branch, weight_out, 1, 0)
        gate_flow.step(grad_branch)
        feed_flow.step(grad_branch)

        grad_proj, grad_logit = attend_bwd(order, projected, logits, saved, grad_attended, quarter)
        grad_proj = after(grad_proj, up_flow.got, feed_flow.got)
        grad_logit = grad_logit[:, 0, :]
        logit_parts = jnp.concatenate(split(reorder(grad_logit, axis=1)), axis=0)
        beta_twice = jnp.concatenate([weight_beta, weight_beta], axis=1)

        def back(ks):
            lower = jnp.concatenate([logit_parts[:, k * quarter : (k + 1) * quarter] for k in ks], axis=1)
            return dot(rows_of(grad_proj, ks), weight_in, 1, 1) + dot(lower, beta_twice, 0, 1)

        back_flow = Flow(summing_hid(back))
        back_flow.step()
        begun = back_flow.sent
        in_flow = scatter_grad(normed, after(grad_proj, begun))
        in_flow.step()
        up_flow.step(begun)
        feed_widths = to_widths(middle + feed_flow.finish(begun))
        back_flow.step()
        handed = back_flow.sent
        grad_normed = back_flow.finish()
        gate_flow.step(handed)
        grad_gain_one, grad_inputs = norm_back(inputs, scale_one, gain_one, grad_normed)
        grad_beta = dot(after(logit_parts, handed), normed, 1, 0)
        grad_beta = grad_beta[:heads] + grad_beta[heads:]
        vectors = jnp.concatenate([grad_gain_one[None], grad_gain_two[None], grad_beta], axis=0)
        count = vectors.shape[0]
        vectors = vectors.reshape(count, dp, wid, shard).transpose(0, 2, 1, 3).reshape(count, wid * dp * shard)
        extra = jnp.concatenate(split(vectors), axis=0)
        extra = jnp.pad(extra, ((0, -(2 * count) % 16), (0, 0)))
        ended = jnp.concatenate([(grad_inputs + grad_middle).astype(BF), extra], axis=0)
        grad_widths = to_widths(ended)
        in_flow.step(ended)
        up_flow.step(grad_widths)
        grad_out = scatter_plain(dot(grad_branch, after(attended, handed), 0, 0, BF))
        out_pieces = gather_hid(after(feed_widths, ended))
        in_pieces = gather_hid(grad_widths)
        arrived = in_pieces[hid // 2]
        in_flow.step(grad_widths)
        passed = in_flow.sent
        grad_gate, grad_up = gate_flow.finish(arrived), up_flow.finish(passed)

        def row_sums(piece):
            both = jnp.sum(piece[:, 0, quarter : quarter + 2 * count].astype(F32), axis=0)
            return (both[:count] + both[count:]).reshape(count, dp, shard)

        sums = [row_sums(p) for p in in_pieces]
        gains = functools.reduce(jnp.add, [one[:2] for one in sums])
        sums = jnp.concatenate([gains, sums[0][2:]], axis=0)
        vectors = lax.dynamic_index_in_dim(sums, me_dp, 1, keepdims=False)
        for by in range(1, dp):
            theirs = lax.dynamic_index_in_dim(sums, (me_dp + by) % dp, 1, keepdims=False)
            vectors = vectors + lax.ppermute(theirs, "dp", [(i, (i + by) % dp) for i in range(dp)])
        in_pieces = [after(p, passed) for p in in_pieces]
        output, grad_input = placed(out_pieces, BF), placed(in_pieces, F32)
        grad_in = in_flow.finish().reshape(shard, heads, 4, HD).transpose(0, 2, 1, 3).reshape(shard, 4, heads * HD)

        return (
            output, grad_input, vectors[0], vectors[1], grad_in, vectors[2:].T, grad_out.T,
            grad_gate, grad_up, grad_down.T,
        )

    return body


def solution(mesh):
    by_rows, by_cols = P(("dp", "wid"), "hid"), P("hid", ("dp", "wid"))
    both = P(("dp", "wid"))
    deep = P(("dp", "wid"), None, "hid")
    wide = P("dp", "wid")
    return jax.shard_map(
        make_body(dict(mesh.shape)),
        mesh=mesh,
        in_specs=(wide, wide, P(("dp", "wid"), None), both, both, deep, by_rows, by_cols, by_rows, by_rows, by_cols),
        out_specs=(wide, wide, both, both, deep, by_rows, by_cols, by_rows, by_rows, by_cols),
        check_vma=False,
    )
```
